32 devices in a mesh: series: 4 (over z), head: 8 (over y, x, core).
Axes of the slice: x: 2, y: 2, z: 4, core: 2. Of those that a mesh axis runs over, the one named last changes fastest.
Arguments:
- teacher_in: bfloat16 [32, 128, 4096], P(('series', 'head')), may hold values from -6 to 6
- teacher_gain: float32 [4096], replicated, may hold values from 0.5 to 1.5
- w_gate: bfloat16 [4096, 8192], P(None, 'head'), may hold values from -0.09375 to 0.09375
- w_up: bfloat16 [4096, 8192], P(None, 'head'), may hold values from -0.09375 to 0.09375
- readout: bfloat16 [8192, 1024], P('head'), may hold values from -0.0625 to 0.0625
- distill_proj: bfloat16 [4096, 1024], P('head'), may hold values from -0.09375 to 0.09375
- building_ids: int32 [32], P(('series', 'head')), may hold values from 0 to 1023
- student_in: bfloat16 [32, 128, 1024], P(('series', 'head')), may hold values from -6 to 6
- embed_rows: bfloat16 [1024, 1024], replicated, may hold values from -4 to 4
- covariates: bfloat16 [1024, 128], replicated, may hold values from -5 to 5
- cov_proj: bfloat16 [128, 1024], replicated, may hold values from -0.5 to 0.5
- student_gain: float32 [1024], replicated, may hold values from 0.25 to 1.75
- w_x: bfloat16 [1024, 2048], replicated, may hold values from -0.1875 to 0.1875
- w_bcdt: bfloat16 [1024, 288], replicated, may hold values from -0.1875 to 0.1875
- conv_w: float32 [4, 2304], replicated, may hold values from -3 to 3
- dt_bias: float32 [32], replicated, may hold values from -1 to 1
- a_log: float32 [32], replicated, may hold values from -6 to -2.5
- d_skip: float32 [32], replicated, may hold values from 0.5 to 1.5
- norm_gain: float32 [2048], replicated, may hold values from 0.25 to 1.75
- w_out: bfloat16 [2048, 1024], replicated, may hold values from -0.125 to 0.125
Outputs:
- grad_bcdt: float32 [1024, 288], P(('series', 'head'))
- grad_conv: float32 [4, 2304], P(None, ('series', 'head'))
- grad_gain: float32 [2048], P(('series', 'head'))
- grad_out: float32 [2048, 1024], P(('series', 'head'))
The draws below stay inside these ranges and needn't reach their ends.
Inputs may be any that keep to these rules, and one draw needn't show every extreme that they name: `building_ids`: building ids index rows of the building tables.
All inputs are finite; a program needn't handle non-finite values.
Results may differ from the reference program's by a relative error of at most 0.013.
The reference program's roundings to bfloat16 on the way count: a program that leaves them out, or rounds other values in their place, can miss the bound.
Values may be sent and summed in bfloat16 or wider, within the bound.
No kernel may reach another device: no remote copies, remote signals or barrier semaphores. Data moves between devices by JAX's collectives and lax.ppermute only.
A program may use at most 128 MiB of HBM per device.

```python
import jax
import jax.numpy as jnp
from jax import lax

D = 4096
FF = 8192
DS = 1024
DI = 2048
NST = 128
NHS = 32
KW = 4
PATCHES = 128
NB = 1024
NCOV = 128
SERIES = 32


def set_ends(values, own_key, low, top_value):
    shape = values.shape
    place = [jax.random.randint(jax.random.fold_in(own_key, axis), (), 0, shape[axis]) for axis in range(len(shape))]
    values = values.at[tuple(place)].set(low)
    longest = shape.index(max(shape))
    place[longest] = (place[longest] + 1) % shape[longest]
    return values.at[tuple(place)].set(top_value)


def block_levels(rng, shape, cuts, least, top_value):
    loudness, own = 1.0, jax.random.fold_in(rng, 6)
    for axis_at, parts in cuts:
        heights = jnp.exp(jax.random.uniform(jax.random.fold_in(own, axis_at), (parts,), jnp.float32, least / len(cuts), top_value / len(cuts)))
        loudness = loudness * jnp.repeat(heights, shape[axis_at] // parts).reshape([-1 if axis == axis_at else 1 for axis in range(len(shape))])
    return loudness


def scatter_about(key, dims, scale, reach, shards=(), held_as=jnp.bfloat16):
    level = block_levels(key, dims, shards, -0.22, 0.18) if shards else 1.0
    array = jax.random.normal(key, dims, jnp.float32) * scale * level
    return jnp.minimum(jnp.maximum(array, -reach), reach).astype(held_as)


def setup_inputs(seed: int = 0) -> dict:
    keys = jax.random.split(jax.random.key(seed), 21)
    teacher_in = scatter_about(keys[0], (SERIES, PATCHES, D), 1.0, 6.0, ((0, 32),))
    teacher_gain = jnp.clip(1.0 + 0.1 * jax.random.normal(keys[1], (D,), jnp.float32), 0.5, 1.5)
    w_gate = scatter_about(keys[2], (D, FF), D ** -0.5, 0.09375, ((1, 8),))
    w_up = scatter_about(keys[3], (D, FF), D ** -0.5, 0.09375, ((1, 8),))
    readout = scatter_about(keys[4], (FF, DS), FF ** -0.5, 0.0625, ((0, 8),))
    distill_proj = scatter_about(keys[5], (D, DS), D ** -0.5, 0.09375, ((0, 8),))
    building_ids = set_ends(jax.random.randint(keys[6], (SERIES,), 0, NB), jax.random.fold_in(keys[6], 1), 0, NB - 1).astype(jnp.int32)
    student_in = scatter_about(keys[7], (SERIES, PATCHES, DS), 1.0, 6.0, ((0, 32),))
    embed_rows = scatter_about(keys[8], (NB, DS), 0.7, 4.0)
    covariates = scatter_about(keys[9], (NB, NCOV), 1.0, 5.0)
    cov_proj = scatter_about(keys[10], (NCOV, DS), NCOV ** -0.5, 0.5)
    student_gain = jnp.clip(1.0 + 0.15 * jax.random.normal(keys[11], (DS,), jnp.float32), 0.25, 1.75)
    w_x = scatter_about(keys[12], (DS, DI), DS ** -0.5, 0.1875)
    w_bcdt = scatter_about(keys[13], (DS, 2 * NST + NHS), DS ** -0.5, 0.1875)
    conv_w = scatter_about(keys[14], (KW, DI + 2 * NST), KW ** -0.5, 3.0, (), jnp.float32)
    dt_bias = jnp.clip(jax.random.uniform(keys[15], (NHS,), jnp.float32, -1.0, 1.0), -1.0, 1.0)
    a_log = jnp.clip(jax.random.uniform(keys[16], (NHS,), jnp.float32, -6.0, -2.5), -6.0, -2.5)
    d_skip = jnp.clip(jax.random.uniform(keys[17], (NHS,), jnp.float32, 0.5, 1.5), 0.5, 1.5)
    norm_gain = jnp.clip(1.0 + 0.15 * jax.random.normal(keys[18], (DI,), jnp.float32), 0.25, 1.75)
    w_out = scatter_about(keys[19], (DI, DS), DI ** -0.5, 0.125)
    return dict(teacher_in=teacher_in, teacher_gain=teacher_gain, w_gate=w_gate, w_up=w_up, readout=readout, distill_proj=distill_proj, building_ids=building_ids, student_in=student_in, embed_rows=embed_rows, covariates=covariates, cov_proj=cov_proj, student_gain=student_gain, w_x=w_x, w_bcdt=w_bcdt, conv_w=conv_w, dt_bias=dt_bias, a_log=a_log, d_skip=d_skip, norm_gain=norm_gain, w_out=w_out)


EPS = 1e-05

def rms_scale(values, gain):
    mean_sq = lax.optimization_barrier(jnp.mean(values * values, axis=-1, keepdims=True))
    return values * lax.rsqrt(mean_sq + EPS) * gain

def teacher_rows(row_block, teacher_gain, w_gate, w_up, readout, proj_rows, feat_start):
    normed = rms_scale(row_block.astype(jnp.float32), teacher_gain).astype(jnp.bfloat16)
    gate_vals = jnp.dot(normed, w_gate, preferred_element_type=jnp.float32)
    upward = jnp.dot(normed, w_up, preferred_element_type=jnp.float32)
    hidden = (jax.nn.silu(gate_vals) * upward).astype(jnp.bfloat16)
    features = lax.dynamic_slice_in_dim(row_block, feat_start, proj_rows.shape[0], 1)
    return jnp.dot(hidden, readout, preferred_element_type=jnp.float32) + jnp.dot(features, proj_rows, preferred_element_type=jnp.float32)

def mixer_core(projected, conv_w, norm_gain, x_stream, dt_bias, a_log, d_skip):
    seq_len = x_stream.shape[0]
    inner_width = x_stream.shape[1]
    head_count = dt_bias.shape[0]
    state_size = (projected.shape[1] - head_count) // 2
    head_size = inner_width // head_count
    mixture = jnp.concatenate([x_stream, projected[:, :2 * state_size]], axis=1)
    taps = conv_w.shape[0]
    padded = jnp.pad(mixture, ((taps - 1, 0), (0, 0)))
    convolved = padded[0:seq_len] * conv_w[0]
    for offset in range(1, taps):
        convolved = convolved + padded[offset:offset + seq_len] * conv_w[offset]
    activated = jax.nn.silu(convolved)
    x_heads = activated[:, :inner_width].reshape(seq_len, head_count, head_size)
    b_state = activated[:, inner_width:inner_width + state_size]
    c_state = activated[:, inner_width + state_size:]
    dt_step = jax.nn.softplus(projected[:, 2 * state_size:] + dt_bias)
    running = jnp.cumsum(dt_step * -jnp.exp(a_log), axis=0)
    later_pos = lax.broadcasted_iota(jnp.int32, (seq_len, seq_len), 0)
    earlier_pos = lax.broadcasted_iota(jnp.int32, (seq_len, seq_len), 1)
    differences = running[:, None, :] - running[None, :, :]
    decays = jnp.exp(jnp.where((later_pos >= earlier_pos)[:, :, None], differences, -1e+30))
    scores = jnp.dot(c_state, b_state.T, precision=lax.Precision.HIGHEST)
    weights = scores[:, :, None] * decays * dt_step[None, :, :]
    mixed = jnp.einsum('tsh,shp->thp', weights, x_heads, precision=lax.Precision.HIGHEST) + d_skip[None, :, None] * x_heads
    return rms_scale(mixed.reshape(seq_len, inner_width), norm_gain)

def student_terms(series_x, extra_row, target_rows, student_gain, w_x, w_bcdt, conv_w, dt_bias, a_log, d_skip, norm_gain, w_out, series_total):
    base = series_x.astype(jnp.float32) + extra_row[None, :]
    normed = rms_scale(base, student_gain).astype(jnp.bfloat16)
    x_stream = jnp.dot(normed, w_x, preferred_element_type=jnp.float32)
    projected = jnp.dot(normed, w_bcdt, preferred_element_type=jnp.float32)

    def forward(proj_in, conv_in, gain_in):
        return mixer_core(proj_in, conv_in, gain_in, x_stream, dt_bias, a_log, d_skip)
    out_norm, pullback = jax.vjp(forward, projected, conv_w, norm_gain)
    rounded = out_norm.astype(jnp.bfloat16)
    output = jnp.dot(rounded, w_out, preferred_element_type=jnp.float32)
    d_output = ((output - target_rows) / series_total).astype(jnp.bfloat16)
    d_norm = jnp.dot(d_output, w_out.T, preferred_element_type=jnp.float32)
    d_proj, g_conv, g_gain = pullback(d_norm)
    g_out = jnp.dot(rounded.T, d_output, preferred_element_type=jnp.float32)
    g_bcdt = jnp.dot(normed.T, d_proj.astype(jnp.bfloat16), preferred_element_type=jnp.float32)
    return (g_bcdt, g_conv, g_gain, g_out)

def reference(teacher_in, teacher_gain, w_gate, w_up, readout, distill_proj, building_ids, student_in, embed_rows, covariates, cov_proj, student_gain, w_x, w_bcdt, conv_w, dt_bias, a_log, d_skip, norm_gain, w_out):
    series_total = teacher_in.shape[0]

    def teacher_one(series_rows):
        return teacher_rows(series_rows, teacher_gain, w_gate, w_up, readout, distill_proj, 0)
    target = lax.map(teacher_one, teacher_in)
    extra = embed_rows[building_ids].astype(jnp.float32) + jnp.dot(covariates[building_ids], cov_proj, preferred_element_type=jnp.float32)

    def accumulate(carry, items):
        series_x, extra_row, target_rows = items
        terms = student_terms(series_x, extra_row, target_rows, student_gain, w_x, w_bcdt, conv_w, dt_bias, a_log, d_skip, norm_gain, w_out, series_total)
        return (jax.tree.map(lambda total, term: total + term, carry, terms), None)
    initial = (jnp.zeros(w_bcdt.shape, jnp.float32), jnp.zeros(conv_w.shape, jnp.float32), jnp.zeros(norm_gain.shape, jnp.float32), jnp.zeros(w_out.shape, jnp.float32))
    totals, unused = lax.scan(accumulate, initial, (student_in, extra, target))
    return (totals[0], totals[1], totals[2], totals[3])
```

```python
import jax
import jax.numpy as jnp
from jax import lax
from jax.sharding import PartitionSpec as P

EPS = 1e-05


def rms_scale(values, gain):
    mean_sq = jnp.mean(values * values, axis=-1, keepdims=True)
    return values * lax.rsqrt(mean_sq + EPS) * gain


def mixer_core(projected, conv_w, norm_gain, x_stream, dt_bias, a_log, d_skip):
    seq_len = x_stream.shape[0]
    inner_width = x_stream.shape[1]
    head_count = dt_bias.shape[0]
    state_size = (projected.shape[1] - head_count) // 2
    head_size = inner_width // head_count
    mixture = jnp.concatenate([x_stream, projected[:, : 2 * state_size]], axis=1)
    taps = conv_w.shape[0]
    padded = jnp.pad(mixture, ((taps - 1, 0), (0, 0)))
    convolved = padded[0:seq_len] * conv_w[0]
    for offset in range(1, taps):
        convolved = convolved + padded[offset : offset + seq_len] * conv_w[offset]
    activated = jax.nn.silu(convolved)
    x_heads = activated[:, :inner_width].reshape(seq_len, head_count, head_size)
    b_state = activated[:, inner_width : inner_width + state_size]
    c_state = activated[:, inner_width + state_size :]
    dt_step = jax.nn.softplus(projected[:, 2 * state_size :] + dt_bias)
    later_pos = lax.broadcasted_iota(jnp.int32, (seq_len, seq_len), 0)
    earlier_pos = lax.broadcasted_iota(jnp.int32, (seq_len, seq_len), 1)
    earlier = (later_pos >= earlier_pos).astype(jnp.float32)
    running = jnp.dot(earlier, dt_step * -jnp.exp(a_log), precision=lax.Precision.HIGHEST)
    differences = running[:, None, :] - running[None, :, :]
    decays = jnp.exp(jnp.where((later_pos >= earlier_pos)[:, :, None], differences, -1e30))
    scores = jnp.dot(c_state, b_state.T, precision=lax.Precision.HIGHEST)
    weights = scores[:, :, None] * decays * dt_step[None, :, :]
    mixed = (
        jnp.einsum("tsh,shp->thp", weights, x_heads, precision=lax.Precision.HIGHEST)
        + d_skip[None, :, None] * x_heads
    )
    return rms_scale(mixed.reshape(seq_len, inner_width), norm_gain)


def swap(values):
    size = lax.axis_size("head")
    return lax.ppermute(values, "head", [(i, i ^ 1) for i in range(size)])


def hop(values, step):
    size = lax.axis_size("head")
    return lax.ppermute(values, "head", [(i, i ^ (2 * step)) for i in range(size)])


def level(values, step):
    size = lax.axis_size("series")
    return lax.ppermute(values, "series", [(i, i ^ step) for i in range(size)])


def teacher_rows(row_block, teacher_gain, w_gate, w_up, readout, proj_rows, feat_start):
    normed = rms_scale(row_block.astype(jnp.float32), teacher_gain).astype(jnp.bfloat16)
    gate_vals = jnp.dot(normed, w_gate, preferred_element_type=jnp.float32)
    upward = jnp.dot(normed, w_up, preferred_element_type=jnp.float32)
    hidden = (jax.nn.silu(gate_vals) * upward).astype(jnp.bfloat16)
    features = lax.dynamic_slice_in_dim(row_block, feat_start, proj_rows.shape[0], 1)
    return jnp.dot(hidden, readout, preferred_element_type=jnp.float32) + jnp.dot(
        features, proj_rows, preferred_element_type=jnp.float32
    )


def gather_blocks(own, chips):
    if chips != 4:
        return [own] + [hop(own, k) for k in range(1, chips)]
    half = own.shape[0] // 2
    top, bottom = own[:half], own[half:]
    x_bottom, y_top = hop(bottom, 1), hop(top, 2)
    x_top, y_bottom = hop(top, 1), hop(bottom, 2)
    diag_top, diag_bottom = hop(y_top, 1), hop(x_bottom, 2)
    return [
        own,
        jnp.concatenate([x_top, x_bottom]),
        jnp.concatenate([y_top, y_bottom]),
        jnp.concatenate([diag_top, diag_bottom]),
    ]


def columns_for(values, chip, chips, levels):
    width = values.shape[1] // (levels * chips)
    return jnp.concatenate(
        [
            lax.dynamic_slice_in_dim(values, (z * chips + chip) * width, width, 1)
            for z in range(levels)
        ],
        axis=1,
    )


def per_device(
    teacher_in, teacher_gain, w_gate, w_up, readout, distill_proj, building_ids, student_in,
    embed_rows, covariates, cov_proj, student_gain, w_x, w_bcdt, conv_w, dt_bias, a_log, d_skip,
    norm_gain, w_out,
):
    heads, levels = lax.axis_size("head"), lax.axis_size("series")
    chips = heads // 2
    head, z = lax.axis_index("head"), lax.axis_index("series")
    chip, core = head // 2, head % 2
    seq_len = teacher_in.shape[1]
    series_total = teacher_in.shape[0] * heads * levels
    bf16, f32 = jnp.bfloat16, jnp.float32

    feat_start = head * distill_proj.shape[0]
    blocks = gather_blocks(teacher_in[0], chips)
    sent = []
    own_part = None
    for k in list(range(1, chips)) + [0]:
        rows = jnp.concatenate([blocks[k], swap(blocks[k])])
        terms = teacher_rows(rows, teacher_gain, w_gate, w_up, readout, distill_proj, feat_start)
        both = terms[:seq_len] + swap(terms[seq_len:].astype(bf16)).astype(f32)
        if k:
            sent.append(hop(both.astype(bf16), k))
        else:
            own_part = both
    target = own_part
    for part in sent:
        target = target + part.astype(f32)

    selector = (
        building_ids[:, None] == lax.broadcasted_iota(jnp.int32, (1, embed_rows.shape[0]), 1)
    ).astype(bf16)
    embedded = jnp.dot(selector, embed_rows, preferred_element_type=f32)
    cov_rows = jnp.dot(selector, covariates, preferred_element_type=f32).astype(bf16)
    extra = embedded + jnp.dot(cov_rows, cov_proj, preferred_element_type=f32)
    base = student_in[0].astype(f32) + extra
    normed = rms_scale(base, student_gain).astype(bf16)
    x_stream = jnp.dot(normed, w_x, preferred_element_type=f32)
    projected = jnp.dot(normed, w_bcdt, preferred_element_type=f32)

    def forward(proj_in, conv_in, gain_in):
        return mixer_core(proj_in, conv_in, gain_in, x_stream, dt_bias, a_log, d_skip)

    out_norm, pullback = jax.vjp(forward, projected, conv_w, norm_gain)
    rounded = out_norm.astype(bf16)
    output = jnp.dot(rounded, w_out, preferred_element_type=f32)

    out_cols = [columns_for(rounded, chip ^ k, chips, levels) for k in range(chips)]
    out_cols = [out_cols[0]] + [hop(out_cols[k], k) for k in range(1, chips)]
    in_cols = [columns_for(normed, chip ^ k, chips, levels) for k in range(chips)]
    in_cols = [in_cols[0]] + [hop(in_cols[k], k) for k in range(1, chips)]

    d_output = ((output - target) / series_total).astype(bf16)
    d_blocks = jnp.concatenate([d_output] + [hop(d_output, k) for k in range(1, chips)])
    d_norm = jnp.dot(d_output, w_out.T, preferred_element_type=f32)
    d_proj, g_conv, g_gain = pullback(d_norm)
    d_proj = d_proj.astype(bf16)
    p_blocks = jnp.concatenate([d_proj] + [hop(d_proj, k) for k in range(1, chips)])

    def pick(values, index, axis):
        return lax.dynamic_index_in_dim(values, index, axis, keepdims=False)

    def spread(part, wire):
        mine = pick(part, core, 1) + swap(pick(part, 1 - core, 1).astype(wire)).astype(f32)
        total = pick(mine, z, 0)
        for k in range(1, levels):
            total = total + level(pick(mine, z ^ k, 0).astype(wire), k).astype(f32)
        return total

    def product(cols, blocks):
        part = lax.dot_general(
            jnp.concatenate(cols), blocks, (((0,), (0,)), ((), ())), preferred_element_type=f32
        )
        return part.reshape(levels, 2, part.shape[0] // (2 * levels), part.shape[1])

    g_out = spread(product(out_cols, d_blocks), bf16)
    g_bcdt = spread(product(in_cols, p_blocks), f32)

    taps, conv_width = g_conv.shape
    terms = jnp.concatenate(
        [
            jnp.moveaxis(g_conv.reshape(taps, levels, chips, 2, -1), 0, 3).reshape(
                levels, chips, 2, -1
            ),
            g_gain.reshape(levels, chips, 2, -1),
        ],
        axis=3,
    )
    part = pick(terms, chip, 1)
    for k in range(1, chips):
        part = part + hop(pick(terms, chip ^ k, 1), k)
    tail = spread(part, f32)
    n_conv = conv_width // (heads * levels)
    return (g_bcdt, tail[: taps * n_conv].reshape(taps, n_conv), tail[taps * n_conv :], g_out)


def solution(mesh):
    return jax.shard_map(
        per_device,
        mesh=mesh,
        in_specs=(
            P(("series", "head"), None, None),
            P(),
            P(None, "head"),
            P(None, "head"),
            P("head", None),
            P("head", None),
            P(("series", "head")),
            P(("series", "head"), None, None),
            P(),
            P(),
            P(),
            P(),
            P(),
            P(),
            P(),
            P(),
            P(),
            P(),
            P(),
            P(),
        ),
        out_specs=(
            P(("series", "head"), None),
            P(None, ("series", "head")),
            P(("series", "head")),
            P(("series", "head"), None),
        ),
        check_vma=False,
    )
```

```python
import jax
import jax.numpy as jnp
from jax import lax
from jax.experimental import pallas as pl
from jax.experimental.pallas import tpu as pltpu
from jax.sharding import PartitionSpec as P

EPS = 1e-05


VMEM = pl.BlockSpec(memory_space=pltpu.VMEM)
SMEM = pl.BlockSpec(memory_space=pltpu.SMEM)
PAIR = 128
TERM_ROWS = 32
TERM_CHUNKS = 6
HEAD, CORE, LEVEL, CHIP, DEVICE = range(5)


def exact_dot(left, right, dims=((1,), (0,))):
    return lax.dot_general(
        left, right, (dims, ((), ())), precision=lax.Precision.HIGHEST,
        preferred_element_type=jnp.float32,
    )


def delayed(values, rows):
    if rows == 0:
        return values
    at = lax.broadcasted_iota(jnp.int32, values.shape, 0)
    return jnp.where(at >= rows, pltpu.roll(values, rows, 0), 0.0)


def advanced(values, rows):
    if rows == 0:
        return values
    size = values.shape[0]
    at = lax.broadcasted_iota(jnp.int32, values.shape, 0)
    return jnp.where(at < size - rows, pltpu.roll(values, size - rows, 0), 0.0)


def head_lanes(head_count, width):
    head = lax.broadcasted_iota(jnp.int32, (head_count, width), 0)
    lane = lax.broadcasted_iota(jnp.int32, (head_count, width), 1)
    size = width // head_count
    return ((lane >= head * size) & (lane < (head + 1) * size)).astype(jnp.float32)


def stacked_by_head(values, head_size):
    lane = lax.broadcasted_iota(jnp.int32, values.shape, 1)
    return jnp.concatenate(
        [
            jnp.where((lane >= at) & (lane < at + head_size), values, 0.0)
            for at in range(0, values.shape[1], head_size)
        ]
    )


def forward_kernel(
    chips, levels, meta, x, emb, cov, cov_proj, s_gain, w_x, w_bcdt, conv_w, dt_bias, a_log, d_skip, n_gain, w_out,
    *refs,
):
    outgoing = refs[:chips]
    (output, mix, slope, xa, dt_wide, y, inv, decay_t, scores_t, bc, dt, gate_dt,
     normed, rounded, sorted_cols) = refs[chips:]
    f32 = jnp.float32
    seq, inner = xa.shape
    heads = dt.shape[1]
    state = bc.shape[1] // 2
    head_size = inner // heads
    extra = emb[...].astype(f32) + jnp.dot(cov[...], cov_proj[...], preferred_element_type=f32)[:1]
    base = x[...].astype(f32) + extra
    mean_sq = jnp.mean(base * base, axis=-1, keepdims=True)
    normed[...] = (base * lax.rsqrt(mean_sq + EPS) * s_gain[...]).astype(jnp.bfloat16)
    projected = jnp.dot(normed[...], w_bcdt[...], preferred_element_type=f32)
    mix[:, :inner] = jnp.dot(normed[...], w_x[...], preferred_element_type=f32)
    mix[:, inner:] = projected[:, : 2 * state]

    taps = conv_w.shape[0]
    for at in range(0, inner + 2 * state, 256):
        cols = slice(at, at + 256)
        values = mix[:, cols]
        conv = values * conv_w[taps - 1 : taps, cols]
        for k in range(taps - 1):
            conv = conv + delayed(values, taps - 1 - k) * conv_w[k : k + 1, cols]
        gate = 1.0 / (1.0 + jnp.exp(-conv))
        slope[:, cols] = gate * (1.0 + conv * (1.0 - gate))
        if at < inner:
            xa[:, cols] = conv * gate
        else:
            bc[:, at - inner : at - inner + 256] = conv * gate

    logits = projected[:, 2 * state : 2 * state + heads] + dt_bias[...]
    steps = jnp.maximum(logits, 0.0) + jnp.log1p(jnp.exp(-jnp.abs(logits)))
    dt[...] = steps
    gate_dt[...] = 1.0 / (1.0 + jnp.exp(-logits))
    row = lax.broadcasted_iota(jnp.int32, (seq, seq), 0)
    col = lax.broadcasted_iota(jnp.int32, (seq, seq), 1)
    running = exact_dot((row >= col).astype(f32), steps * -jnp.exp(a_log[...]))
    running_t = jnp.concatenate([running, jnp.zeros((seq, 128 - heads), f32)], axis=1).T
    lanes = head_lanes(heads, inner)
    dt_wide[...] = exact_dot(steps, lanes)
    scores = exact_dot(bc[:, state:], bc[:, :state], ((1,), (1,)))
    scores_t[...] = scores.T

    group = PAIR // head_size
    for p in range(inner // PAIR):
        cols = slice(p * PAIR, (p + 1) * PAIR)
        weights = []
        for h in range(p * group, (p + 1) * group):
            down, across = running[:, h : h + 1], running_t[h : h + 1, :]
            decay = jnp.exp(jnp.where(row >= col, down - across, -1e30))
            decay_t[h] = jnp.exp(jnp.where(col >= row, across - down, -1e30))
            weights.append(scores * decay)
        held = stacked_by_head(dt_wide[:, cols] * xa[:, cols], head_size)
        y[:, cols] = exact_dot(jnp.concatenate(weights, axis=1), held)

    skip = exact_dot(jnp.broadcast_to(d_skip[...], (8, heads)), lanes)[:1]
    mixed = y[...] + skip * xa[...]
    scale = lax.rsqrt(jnp.mean(mixed * mixed, axis=-1, keepdims=True) + EPS)
    inv[...] = jnp.broadcast_to(scale, inv.shape)
    rounded[...] = (mixed * scale * n_gain[...]).astype(jnp.bfloat16)
    output[...] = jnp.dot(rounded[...], w_out[...], preferred_element_type=f32)

    start = 0
    for values in (rounded, normed):
        width = values.shape[1] // (levels * chips)
        for z in range(levels):
            for chip in range(chips):
                at = (z * chips + chip) * width
                sorted_cols[chip, :, start : start + width] = values[:, at : at + width]
            start += width
    for k in range(chips):
        outgoing[k][...] = sorted_cols[meta[CHIP] ^ k]


def backward_kernel(
    d_out, w_out, n_gain, conv_w, a_log, d_skip, mix, slope, xa, dt_wide, y, inv, decay_t, scores_t,
    bc, dt, gate_dt, message, g_conv, d_mixed, through,
):
    f32 = jnp.float32
    seq, inner = xa.shape
    heads = dt.shape[1]
    state = bc.shape[1] // 2
    head_size = inner // heads
    taps = conv_w.shape[0]
    lanes = head_lanes(heads, inner)
    skip = exact_dot(jnp.broadcast_to(d_skip[...], (8, heads)), lanes)[:1]
    scale = inv[:, :1]
    d_norm = lax.dot_general(
        d_out[...], w_out[...], (((1,), (1,)), ((), ())), preferred_element_type=f32
    )
    unit = (y[...] + skip * xa[...]) * scale
    wide = message.shape[1]
    bf16 = jnp.bfloat16
    message[...] = jnp.zeros_like(message)
    g_conv[...] = jnp.zeros_like(g_conv)
    g_conv[taps : taps + 1, :inner] = jnp.sum(d_norm * unit, axis=0, keepdims=True)
    pulled = d_norm * n_gain[...]
    d_mixed[...] = scale * (pulled - unit * jnp.mean(pulled * unit, axis=-1, keepdims=True))

    group = PAIR // head_size
    d_scores_t = jnp.zeros((seq, seq), f32)
    scored = scores_t[...]
    for p in range(inner // PAIR):
        cols = slice(p * PAIR, (p + 1) * PAIR)
        got = d_mixed[:, cols]
        held = dt_wide[:, cols] * xa[:, cols]
        weights = jnp.concatenate(
            [scored * decay_t[h] for h in range(p * group, (p + 1) * group)], axis=1
        )
        through[:, cols] = exact_dot(weights, stacked_by_head(got, head_size))
        outer = exact_dot(stacked_by_head(held, head_size), got, ((1,), (1,)))
        for i in range(group):
            d_scores_t = d_scores_t + outer[i * seq : (i + 1) * seq] * decay_t[p * group + i]

    d_dt = exact_dot(through[...] * xa[...], lanes, ((1,), (1,)))
    d_running = exact_dot(d_mixed[...] * y[...], lanes, ((1,), (1,))) - dt[...] * d_dt
    row = lax.broadcasted_iota(jnp.int32, (seq, seq), 0)
    col = lax.broadcasted_iota(jnp.int32, (seq, seq), 1)
    later = exact_dot((col >= row).astype(f32), d_running)
    d_step = (d_dt + later * -jnp.exp(a_log[...])) * gate_dt[...]

    for at in range(0, inner, 256):
        cols = slice(at, at + 256)
        d_act = dt_wide[:, cols] * through[:, cols] + skip[:, cols] * d_mixed[:, cols]
        d_conv = d_act * slope[:, cols]
        values = mix[:, cols]
        for k in range(taps):
            g_conv[k : k + 1, cols] = jnp.sum(
                d_conv * delayed(values, taps - 1 - k), axis=0, keepdims=True
            )
    d_b = exact_dot(d_scores_t, bc[:, state:])
    d_c = exact_dot(d_scores_t.T, bc[:, :state])
    for at, d_act in ((0, d_b), (state, d_c)):
        cols = slice(inner + at, inner + at + state)
        d_conv = d_act * slope[:, cols]
        values = mix[:, cols]
        d_mix = d_conv * conv_w[taps - 1 : taps, cols]
        for k in range(taps):
            g_conv[k : k + 1, cols] = jnp.sum(
                d_conv * delayed(values, taps - 1 - k), axis=0, keepdims=True
            )
            if k < taps - 1:
                d_mix = d_mix + advanced(d_conv, taps - 1 - k) * conv_w[k : k + 1, cols]
        message[:seq, at : at + state] = d_mix.astype(bf16)
    message[:seq, 2 * state : 2 * state + heads] = d_step.astype(bf16)
    per_row = (inner + 2 * state) // wide
    packed = [
        g_conv[k : k + 1, i * wide : (i + 1) * wide] for k in range(taps + 1) for i in range(per_row)
    ]
    packed = packed + [jnp.zeros_like(packed[0])] * (TERM_ROWS - len(packed))
    message[seq:, :] = jnp.concatenate(packed).astype(bf16)


def cost(micros):
    return pl.CostEstimate(flops=int(micros * 1e9), transcendentals=0, bytes_accessed=0)


def pinned(shape, dtype):
    return pltpu.VMEM(shape, dtype)


def load_kernel(count, *refs):
    sems = refs[2 * count]
    copies = [pltpu.make_async_copy(refs[i], refs[count + i], sems.at[i]) for i in range(count)]
    for copy in copies:
        copy.start()
    for copy in copies:
        copy.wait()


def load(values):
    count = len(values)
    return pl.pallas_call(
        lambda *refs: load_kernel(count, *refs),
        name="load",
        in_specs=[pl.BlockSpec(memory_space=pltpu.HBM)] * count,
        out_specs=[VMEM] * count,
        out_shape=[pinned(v.shape, v.dtype) for v in values],
        scratch_shapes=[pltpu.SemaphoreType.DMA((count,))],
        compiler_params=pltpu.CompilerParams(vmem_limit_bytes=1 << 20),
        cost_estimate=cost(6),
    )(*[pltpu.with_memory_space_constraint(v, pltpu.HBM) for v in values])


def in_vmem(values):
    return [pltpu.with_memory_space_constraint(v, pltpu.VMEM) for v in values]


def student_forward(chips, levels, meta, x, emb, cov, cov_proj, s_gain, w_x, w_bcdt, conv_w, dt_bias, a_log, d_skip, n_gain, w_out):
    seq, width = x.shape
    inner, heads = w_x.shape[1], dt_bias.shape[1]
    both = conv_w.shape[1]
    f32, bf16 = jnp.float32, jnp.bfloat16
    wide = (inner + width) // chips
    shapes = [((seq, wide), bf16)] * chips + [
        ((seq, w_out.shape[1]), f32),
        ((seq, both), f32), ((seq, both), f32), ((seq, inner), f32), ((seq, inner), f32),
        ((seq, inner), f32), ((seq, 128), f32), ((heads, seq, seq), f32), ((seq, seq), f32),
        ((seq, both - inner), f32), ((seq, heads), f32), ((seq, heads), f32),
    ]
    return pl.pallas_call(
        lambda *refs: forward_kernel(chips, levels, *refs),
        name="student_forward",
        in_specs=[SMEM] + [VMEM] * 13,
        out_specs=[VMEM] * len(shapes),
        out_shape=[jax.ShapeDtypeStruct(s, t) for s, t in shapes[:chips]]
        + [pinned(s, t) for s, t in shapes[chips:]],
        scratch_shapes=[
            pltpu.VMEM((seq, width), bf16), pltpu.VMEM((seq, inner), bf16),
            pltpu.VMEM((chips, seq, wide), bf16),
        ],
        compiler_params=pltpu.CompilerParams(vmem_limit_bytes=14 << 20),
        cost_estimate=cost(6),
    )(meta, x, emb, cov, cov_proj, s_gain, w_x, w_bcdt, conv_w, dt_bias, a_log, d_skip, n_gain, *in_vmem([w_out]))


def student_backward(d_out, w_out, n_gain, conv_w, a_log, d_skip, saved):
    seq = d_out.shape[0]
    inner, heads = w_out.shape[0], a_log.shape[1]
    both = conv_w.shape[1]
    f32 = jnp.float32
    wide = both // TERM_CHUNKS
    return pl.pallas_call(
        backward_kernel,
        name="student_backward",
        in_specs=[VMEM] * (6 + len(saved)),
        out_specs=VMEM,
        out_shape=jax.ShapeDtypeStruct((seq + TERM_ROWS, wide), jnp.bfloat16),
        scratch_shapes=[
            pltpu.VMEM((8, both), f32), pltpu.VMEM((seq, inner), f32), pltpu.VMEM((seq, inner), f32),
        ],
        compiler_params=pltpu.CompilerParams(vmem_limit_bytes=14 << 20),
        cost_estimate=cost(9),
    )(d_out, *in_vmem([w_out]), n_gain, conv_w, a_log, d_skip, *in_vmem(saved))


def contract_kernel(count, lanes, extra, meta, *refs):
    cols, blocks = refs[:count], refs[count : 2 * count]
    mine, theirs, part = refs[2 * count :]
    f32 = jnp.float32
    seq = cols[0].shape[0]
    part[...] = lax.dot_general(
        jnp.concatenate([c[:, lanes] for c in cols]),
        jnp.concatenate([b[:seq, :] for b in blocks]),
        (((0,), (0,)), ((), ())),
        preferred_element_type=f32,
    ).reshape(part.shape)
    rows = part.shape[0] * part.shape[2]
    width = part.shape[3]
    mine[:rows, :] = part[:, pl.ds(meta[CORE], 1), :, :].reshape(rows, width)
    theirs[:rows, :] = part[:, pl.ds(1 - meta[CORE], 1), :, :].reshape(rows, width).astype(theirs.dtype)
    if extra:
        total = blocks[0][seq:, :].astype(f32)
        for block in blocks[1:]:
            total = total + block[seq:, :].astype(f32)
        mine[rows:, :] = total
        theirs[rows:, :] = total.astype(theirs.dtype)


def contract(meta, cols, lanes, blocks, levels):
    count = len(cols)
    width = blocks[0].shape[1]
    extra = blocks[0].shape[0] - cols[0].shape[0]
    own = (lanes.stop - lanes.start) // (2 * levels)
    rows = levels * own + extra
    return pl.pallas_call(
        lambda *refs: contract_kernel(count, lanes, extra, *refs),
        name="contract",
        in_specs=[SMEM] + [VMEM] * (2 * count),
        out_specs=[VMEM, VMEM],
        out_shape=[
            jax.ShapeDtypeStruct((rows, width), jnp.float32),
            jax.ShapeDtypeStruct((rows, width), jnp.bfloat16),
        ],
        scratch_shapes=[pltpu.VMEM((levels, 2, own, width), jnp.float32)],
        compiler_params=pltpu.CompilerParams(vmem_limit_bytes=14 << 20),
        cost_estimate=cost(2),
    )(meta, *cols, *blocks)


def share_kernel(levels, extra, meta, mine, got, own, *sent):
    rows = (mine.shape[0] - extra) // levels
    for k, to in ((0, own), *((i + 1, m) for i, m in enumerate(sent))):
        at = pl.multiple_of((meta[LEVEL] ^ k) * rows, rows)
        total = mine[pl.ds(at, rows), :] + got[pl.ds(at, rows), :].astype(jnp.float32)
        to[:rows, :] = total.astype(to.dtype)
        if extra:
            tail = slice(mine.shape[0] - extra, mine.shape[0])
            to[rows:, :] = (mine[tail, :] + got[tail, :].astype(jnp.float32)).astype(to.dtype)


def share(meta, mine, got, levels, extra):
    rows = (mine.shape[0] - extra) // levels + extra
    width = mine.shape[1]
    return pl.pallas_call(
        lambda *refs: share_kernel(levels, extra, *refs),
        name="share",
        in_specs=[SMEM, VMEM, VMEM],
        out_specs=[VMEM] * levels,
        out_shape=[jax.ShapeDtypeStruct((rows, width), jnp.float32)]
        + [jax.ShapeDtypeStruct((rows, width), jnp.bfloat16)] * (levels - 1),
        compiler_params=pltpu.CompilerParams(vmem_limit_bytes=14 << 20),
        cost_estimate=cost(1),
    )(meta, mine, got)


def finish_kernel(count, taps, meta, own_a, own_b, *refs):
    got_a, got_b = refs[:count], refs[count : 2 * count]
    g_bcdt, g_conv, g_gain, g_out, terms = refs[2 * count :]
    f32 = jnp.float32
    total = own_a[...]
    for part in got_a:
        total = total + part[...].astype(f32)
    g_out[...] = total
    total = own_b[...]
    for part in got_b:
        total = total + part[...].astype(f32)
    rows, wide = g_bcdt.shape[0], total.shape[1]
    g_bcdt[...] = total[:rows, : g_bcdt.shape[1]]
    terms[...] = total[rows:, :]
    lane = lax.broadcasted_iota(jnp.int32, (1, wide), 1)

    def window(first, width):
        start = meta[DEVICE] * width
        chunk = start // wide
        offset = start - chunk * wide
        left = pltpu.roll(terms[pl.ds(first + chunk, 1), :], wide - offset, 1)
        right = pltpu.roll(terms[pl.ds(first + chunk + 1, 1), :], wide - offset, 1)
        return jnp.where(lane < wide - offset, left, right)[:, :width]

    g_conv[...] = jnp.concatenate(
        [window(k * TERM_CHUNKS, g_conv.shape[1]) for k in range(taps)]
    )
    g_gain[...] = window(taps * TERM_CHUNKS, g_gain.shape[1])


def finish(meta, own_a, own_b, got_a, got_b, shapes):
    f32 = jnp.float32
    return pl.pallas_call(
        lambda *refs: finish_kernel(len(got_a), shapes[1][0], *refs),
        name="finish",
        in_specs=[SMEM] + [VMEM] * (2 + len(got_a) + len(got_b)),
        out_specs=[VMEM] * 4,
        out_shape=[jax.ShapeDtypeStruct(s, f32) for s in shapes],
        scratch_shapes=[pltpu.VMEM((TERM_ROWS, own_b.shape[1]), f32)],
        compiler_params=pltpu.CompilerParams(vmem_limit_bytes=14 << 20),
        cost_estimate=cost(2),
    )(meta, own_a, own_b, *got_a, *got_b)


def swap(values):
    size = lax.axis_size("head")
    return lax.ppermute(values, "head", [(i, i ^ 1) for i in range(size)])


def hop(values, step):
    size = lax.axis_size("head")
    return lax.ppermute(values, "head", [(i, i ^ (2 * step)) for i in range(size)])


def level(values, step):
    size = lax.axis_size("series")
    return lax.ppermute(values, "series", [(i, i ^ step) for i in range(size)])


def teacher_kernel(count, meta, *refs):
    pieces = refs[:count]
    gain, w_gate, w_up, readout, proj, mine, theirs, normed, acc = refs[count:]
    f32 = jnp.float32
    feat = proj.shape[0]
    feat_at = pl.multiple_of(meta[HEAD] * feat, feat)
    strip = 16
    start = 0
    for piece in pieces:
        for at in range(0, piece.shape[0], strip):
            values = piece[at : at + strip, :].astype(f32)
            mean_sq = jnp.mean(values * values, axis=-1, keepdims=True)
            scaled = values * lax.rsqrt(mean_sq + EPS) * gain[...]
            normed[start + at : start + at + strip, :] = scaled.astype(jnp.bfloat16)
        acc[start : start + piece.shape[0], :] = jnp.dot(
            piece[:, pl.ds(feat_at, feat)], proj[...], preferred_element_type=f32
        )
        start += piece.shape[0]
    tile = min(256, w_gate.shape[1])
    for at in range(0, w_gate.shape[1], tile):
        cols = slice(at, at + tile)
        gate = jnp.dot(normed[...], w_gate[:, cols], preferred_element_type=f32)
        upward = jnp.dot(normed[...], w_up[:, cols], preferred_element_type=f32)
        hidden = (gate / (1.0 + jnp.exp(-gate)) * upward).astype(jnp.bfloat16)
        acc[...] += jnp.dot(hidden, readout[cols, :], preferred_element_type=f32)
    rows = mine.shape[0]
    mine[...] = acc[:rows, :]
    theirs[...] = acc[rows:, :].astype(jnp.bfloat16)


def teacher_terms(meta, own, other, teacher_gain, w_gate, w_up, readout, proj):
    pieces = own + other
    rows = sum(p.shape[0] for p in own)
    width, out = w_gate.shape[0], readout.shape[1]
    return pl.pallas_call(
        lambda *refs: teacher_kernel(len(pieces), *refs),
        name="teacher",
        in_specs=[SMEM] + [VMEM] * (len(pieces) + 5),
        out_specs=[VMEM, VMEM],
        out_shape=[
            jax.ShapeDtypeStruct((rows, out), jnp.float32),
            jax.ShapeDtypeStruct((rows, out), jnp.bfloat16),
        ],
        scratch_shapes=[
            pltpu.VMEM((2 * rows, width), jnp.bfloat16),
            pltpu.VMEM((2 * rows, out), jnp.float32),
        ],
        compiler_params=pltpu.CompilerParams(vmem_limit_bytes=14 << 20),
        cost_estimate=cost(rows / 32),
    )(meta, *pieces, teacher_gain.reshape(1, width), *in_vmem([w_gate, w_up, readout, proj]))


def per_device(
    teacher_in, teacher_gain, w_gate, w_up, readout, distill_proj, building_ids, student_in,
    embed_rows, covariates, cov_proj, student_gain, w_x, w_bcdt, conv_w, dt_bias, a_log, d_skip,
    norm_gain, w_out,
):
    heads, levels = lax.axis_size("head"), lax.axis_size("series")
    chips = heads // 2
    head, z = lax.axis_index("head"), lax.axis_index("series")
    chip, core = head // 2, head % 2
    seq_len = teacher_in.shape[1]
    series_total = teacher_in.shape[0] * heads * levels
    bf16, f32 = jnp.bfloat16, jnp.float32

    own_rows = teacher_in[0]
    across = [hop(own_rows, k) for k in ((1, 2) if chips == 4 else range(1, chips))]
    meta = jnp.stack([head, core, z, chip, z * heads + head]).astype(jnp.int32)
    emb = lax.dynamic_slice_in_dim(embed_rows, building_ids[0], 1, 0)
    cov = lax.dynamic_slice_in_dim(covariates, building_ids[0], 1, 0)
    wide = conv_w.shape[1] // TERM_CHUNKS
    padded = jnp.pad(w_bcdt, ((0, 0), (0, wide - w_bcdt.shape[1])))
    meta, emb, cov, padded, w_gate = lax.optimization_barrier((meta, emb, cov, padded, w_gate))
    w_gate, w_up, readout, distill_proj, w_out = load([w_gate, w_up, readout, distill_proj, w_out])

    def teach(own):
        return teacher_terms(
            meta, own, [swap(p) for p in own], teacher_gain, w_gate, w_up, readout, distill_proj
        )

    first = teach([own_rows])
    row = [v.reshape(1, -1) for v in (student_gain, dt_bias, a_log, d_skip, norm_gain)]
    fwd = student_forward(
        chips, levels, meta, student_in[0], emb, cov, cov_proj, row[0], w_x, padded, conv_w, row[1], row[2], row[3], row[4], w_out
    )
    cols, output, saved = list(fwd[:chips]), fwd[chips], fwd[chips + 1 :]
    across, first, cols = lax.optimization_barrier((across, first, cols))

    def settle(terms, steps):
        mine, theirs = terms
        both = mine + swap(theirs).astype(f32)
        blocks = [both[i * seq_len : (i + 1) * seq_len] for i in range(len(steps))]
        return [hop(v.astype(bf16), k) if k else v for v, k in zip(blocks, steps)]

    def exchanged():
        return [cols[0]] + [hop(cols[k], k) for k in range(1, chips)]

    if chips == 4:
        half = seq_len // 2
        corner = [hop(across[1][:half], 1), hop(across[0][half:], 2)]
        second = teach(across)
        corner, second, cols = lax.optimization_barrier((corner, second, cols))
        parts = settle(first, (0,)) + settle(second, (1, 2))
        third = teach(corner)
        cols = exchanged()
        third, cols = lax.optimization_barrier((third, cols))
        parts = parts + settle(third, (3,))
    else:
        cols = exchanged()
        parts = settle(first, (0,))
        for k, v in enumerate(across):
            parts = parts + settle(teach([v]), (k + 1,))
    parts, cols = lax.optimization_barrier((parts, cols))
    target = parts[0]
    for part in parts[1:]:
        target = target + part.astype(f32)
    split = w_x.shape[1] // chips

    d_output = ((output - target) / series_total).astype(bf16)
    d_blocks = [d_output] + [hop(d_output, k) for k in range(1, chips)]
    message = student_backward(d_output, w_out, row[4], conv_w, row[2], row[3], saved)
    d_blocks, message = lax.optimization_barrier((d_blocks, message))

    messages = [message] + [hop(message, k) for k in range(1, chips)]
    mine, theirs = contract(meta, cols, slice(0, split), d_blocks, levels)
    own_a, *sent_a = share(meta, mine, swap(theirs), levels, 0)
    messages, sent_a = lax.optimization_barrier((messages, sent_a))
    got_a = [level(v, k + 1) for k, v in enumerate(sent_a)]
    mine, theirs = contract(meta, cols, slice(split, cols[0].shape[1]), messages, levels)
    own_b, *sent_b = share(meta, mine, swap(theirs), levels, TERM_ROWS)
    got_b = [level(v, k + 1) for k, v in enumerate(sent_b)]

    devices = heads * levels
    g_bcdt, g_conv, g_gain, g_out = finish(
        meta, own_a, own_b, got_a, got_b,
        [
            (w_bcdt.shape[0] // devices, w_bcdt.shape[1]), (conv_w.shape[0], conv_w.shape[1] // devices),
            (1, norm_gain.shape[0] // devices), (w_out.shape[0] // devices, w_out.shape[1]),
        ],
    )
    return (g_bcdt, g_conv, g_gain.reshape(-1), g_out)


def solution(mesh):
    return jax.shard_map(
        per_device,
        mesh=mesh,
        in_specs=(
            P(("series", "head"), None, None),
            P(),
            P(None, "head"),
            P(None, "head"),
            P("head", None),
            P("head", None),
            P(("series", "head")),
            P(("series", "head"), None, None),
            P(),
            P(),
            P(),
            P(),
            P(),
            P(),
            P(),
            P(),
            P(),
            P(),
            P(),
            P(),
        ),
        out_specs=(
            P(("series", "head"), None),
            P(None, ("series", "head")),
            P(("series", "head")),
            P(("series", "head"), None),
        ),
        check_vma=False,
    )
```

```python
import jax
import jax.numpy as jnp
from jax import lax
from jax.experimental import pallas as pl
from jax.experimental.pallas import tpu as pltpu
from jax.sharding import PartitionSpec as P

EPS = 1e-05


VMEM = pl.BlockSpec(memory_space=pltpu.VMEM)
SMEM = pl.BlockSpec(memory_space=pltpu.SMEM)
PAIR = 128
TERM_ROWS = 32
TERM_CHUNKS = 6
LOADS, INPUTS = 5, 12
HEAD, CORE, LEVEL, CHIP, DEVICE = range(5)


def exact_dot(left, right, dims=((1,), (0,))):
    return lax.dot_general(
        left, right, (dims, ((), ())), precision=lax.Precision.HIGHEST,
        preferred_element_type=jnp.float32,
    )


def halves(values):
    high = values.astype(jnp.bfloat16)
    return high, (values - high.astype(jnp.float32)).astype(jnp.bfloat16)


def close_dot(left, right, dims=((1,), (0,))):
    (lh, ll), (rh, rl) = halves(left), halves(right)

    def dot(a, b):
        return lax.dot_general(a, b, (dims, ((), ())), preferred_element_type=jnp.float32)

    return dot(lh, rh) + (dot(lh, rl) + dot(ll, rh))


def delayed(values, rows):
    if rows == 0:
        return values
    at = lax.broadcasted_iota(jnp.int32, values.shape, 0)
    return jnp.where(at >= rows, pltpu.roll(values, rows, 0), 0.0)


def advanced(values, rows):
    if rows == 0:
        return values
    size = values.shape[0]
    at = lax.broadcasted_iota(jnp.int32, values.shape, 0)
    return jnp.where(at < size - rows, pltpu.roll(values, size - rows, 0), 0.0)


def head_lanes(head_count, width):
    head = lax.broadcasted_iota(jnp.int32, (head_count, width), 0)
    lane = lax.broadcasted_iota(jnp.int32, (head_count, width), 1)
    size = width // head_count
    return ((lane >= head * size) & (lane < (head + 1) * size)).astype(jnp.float32)


def stacked_by_head(values, head_size):
    lane = lax.broadcasted_iota(jnp.int32, values.shape, 1)
    return jnp.concatenate(
        [
            jnp.where((lane >= at) & (lane < at + head_size), values, 0.0)
            for at in range(0, values.shape[1], head_size)
        ]
    )


def forward_kernel(
    chips, levels, meta, *refs
):
    far, refs = refs[: INPUTS + LOADS], refs[INPUTS + LOADS :]
    near, refs = list(refs[:LOADS]), refs[LOADS:]
    held, sems, refs = list(refs[-INPUTS - 1 : -1]), refs[-1], refs[: -INPUTS - 1]
    loads = [pltpu.make_async_copy(f, n, sems.at[i]) for i, (f, n) in enumerate(zip(far, held + near))]
    for copy in loads[:INPUTS]:
        copy.start()
    for copy in loads[:INPUTS]:
        copy.wait()
    loads = loads[INPUTS:]
    for copy in loads:
        copy.start()
    x, emb, cov, cov_proj, s_gain, w_x, w_bcdt, conv_w, dt_bias, a_log, d_skip, n_gain = held
    w_out = near[0]
    outgoing = refs[:chips]
    (output, mix, slope, xa, dt_wide, y, inv, decay_t, scores_t, bc, dt, gate_dt,
     normed, rounded, sorted_cols) = refs[chips:]
    f32 = jnp.float32
    seq, inner = xa.shape
    heads = dt.shape[1]
    state = bc.shape[1] // 2
    head_size = inner // heads
    extra = emb[...].astype(f32) + jnp.dot(cov[...], cov_proj[...], preferred_element_type=f32)[:1]
    base = x[...].astype(f32) + extra
    mean_sq = jnp.mean(base * base, axis=-1, keepdims=True)
    normed[...] = (base * lax.rsqrt(mean_sq + EPS) * s_gain[...]).astype(jnp.bfloat16)
    projected = lax.dot_general(
        normed[...], w_bcdt[...], (((1,), (1,)), ((), ())), preferred_element_type=f32
    )
    mix[:, :inner] = jnp.dot(normed[...], w_x[...], preferred_element_type=f32)
    mix[:, inner:] = projected[:, : 2 * state]

    taps = conv_w.shape[0]
    for at in range(0, inner + 2 * state, 256):
        cols = slice(at, at + 256)
        values = mix[:, cols]
        conv = values * conv_w[taps - 1 : taps, cols]
        for k in range(taps - 1):
            conv = conv + delayed(values, taps - 1 - k) * conv_w[k : k + 1, cols]
        gate = 1.0 / (1.0 + jnp.exp(-conv))
        slope[:, cols] = gate * (1.0 + conv * (1.0 - gate))
        if at < inner:
            xa[:, cols] = conv * gate
        else:
            bc[:, at - inner : at - inner + 256] = conv * gate

    logits = projected[:, 2 * state : 2 * state + heads] + dt_bias[...]
    steps = jnp.maximum(logits, 0.0) + jnp.log1p(jnp.exp(-jnp.abs(logits)))
    dt[...] = steps
    gate_dt[...] = 1.0 / (1.0 + jnp.exp(-logits))
    row = lax.broadcasted_iota(jnp.int32, (seq, seq), 0)
    col = lax.broadcasted_iota(jnp.int32, (seq, seq), 1)
    running = exact_dot((row >= col).astype(f32), steps * -jnp.exp(a_log[...]))
    running_t = jnp.concatenate([running, jnp.zeros((seq, 128 - heads), f32)], axis=1).T
    lanes = head_lanes(heads, inner)
    dt_wide[...] = exact_dot(steps, lanes)
    scores = exact_dot(bc[:, state:], bc[:, :state], ((1,), (1,)))
    scores_t[...] = scores.T

    group = PAIR // head_size
    for p in range(inner // PAIR):
        cols = slice(p * PAIR, (p + 1) * PAIR)
        weights = []
        for h in range(p * group, (p + 1) * group):
            down, across = running[:, h : h + 1], running_t[h : h + 1, :]
            decay = jnp.exp(jnp.where(row >= col, down - across, -1e30))
            decay_t[h] = jnp.exp(jnp.where(col >= row, across - down, -1e30))
            weights.append(scores * decay)
        held = stacked_by_head(dt_wide[:, cols] * xa[:, cols], head_size)
        y[:, cols] = close_dot(jnp.concatenate(weights, axis=1), held)

    skip = exact_dot(jnp.broadcast_to(d_skip[...], (8, heads)), lanes)[:1]
    mixed = y[...] + skip * xa[...]
    scale = lax.rsqrt(jnp.mean(mixed * mixed, axis=-1, keepdims=True) + EPS)
    inv[...] = jnp.broadcast_to(scale, inv.shape)
    rounded[...] = (mixed * scale * n_gain[...]).astype(jnp.bfloat16)
    loads[0].wait()
    output[...] = jnp.dot(rounded[...], w_out[...], preferred_element_type=f32)

    start = 0
    for values in (rounded, normed):
        width = values.shape[1] // (levels * chips)
        for z in range(levels):
            for chip in range(chips):
                at = (z * chips + chip) * width
                sorted_cols[chip, :, start : start + width] = values[:, at : at + width]
            start += width
    for k in range(chips):
        outgoing[k][...] = sorted_cols[meta[CHIP] ^ k]
    for copy in loads[1:]:
        copy.wait()


def backward_kernel(
    d_out, w_out, n_gain, conv_w, a_log, d_skip, mix, slope, xa, dt_wide, y, inv, decay_t, scores_t,
    bc, dt, gate_dt, message, g_conv, d_mixed, through,
):
    f32 = jnp.float32
    seq, inner = xa.shape
    heads = dt.shape[1]
    state = bc.shape[1] // 2
    head_size = inner // heads
    taps = conv_w.shape[0]
    lanes = head_lanes(heads, inner)
    skip = exact_dot(jnp.broadcast_to(d_skip[...], (8, heads)), lanes)[:1]
    scale = inv[:, :1]
    d_norm = lax.dot_general(
        d_out[...], w_out[...], (((1,), (1,)), ((), ())), preferred_element_type=f32
    )
    unit = (y[...] + skip * xa[...]) * scale
    wide = message.shape[1]
    bf16 = jnp.bfloat16
    message[...] = jnp.zeros_like(message)
    g_conv[...] = jnp.zeros_like(g_conv)
    g_conv[taps : taps + 1, :inner] = jnp.sum(d_norm * unit, axis=0, keepdims=True)
    pulled = d_norm * n_gain[...]
    d_mixed[...] = scale * (pulled - unit * jnp.mean(pulled * unit, axis=-1, keepdims=True))

    group = PAIR // head_size
    d_scores_t = jnp.zeros((seq, seq), f32)
    scored = scores_t[...]
    for p in range(inner // PAIR):
        cols = slice(p * PAIR, (p + 1) * PAIR)
        got = d_mixed[:, cols]
        held = dt_wide[:, cols] * xa[:, cols]
        weights = jnp.concatenate(
            [scored * decay_t[h] for h in range(p * group, (p + 1) * group)], axis=1
        )
        through[:, cols] = close_dot(weights, stacked_by_head(got, head_size))
        outer = close_dot(stacked_by_head(held, head_size), got, ((1,), (1,)))
        for i in range(group):
            d_scores_t = d_scores_t + outer[i * seq : (i + 1) * seq] * decay_t[p * group + i]

    d_dt = exact_dot(through[...] * xa[...], lanes, ((1,), (1,)))
    d_running = exact_dot(d_mixed[...] * y[...], lanes, ((1,), (1,))) - dt[...] * d_dt
    row = lax.broadcasted_iota(jnp.int32, (seq, seq), 0)
    col = lax.broadcasted_iota(jnp.int32, (seq, seq), 1)
    later = exact_dot((col >= row).astype(f32), d_running)
    d_step = (d_dt + later * -jnp.exp(a_log[...])) * gate_dt[...]

    for at in range(0, inner, 256):
        cols = slice(at, at + 256)
        d_act = dt_wide[:, cols] * through[:, cols] + skip[:, cols] * d_mixed[:, cols]
        d_conv = d_act * slope[:, cols]
        values = mix[:, cols]
        for k in range(taps):
            g_conv[k : k + 1, cols] = jnp.sum(
                d_conv * delayed(values, taps - 1 - k), axis=0, keepdims=True
            )
    d_b = exact_dot(d_scores_t, bc[:, state:])
    d_c = exact_dot(d_scores_t.T, bc[:, :state])
    for at, d_act in ((0, d_b), (state, d_c)):
        cols = slice(inner + at, inner + at + state)
        d_conv = d_act * slope[:, cols]
        values = mix[:, cols]
        d_mix = d_conv * conv_w[taps - 1 : taps, cols]
        for k in range(taps):
            g_conv[k : k + 1, cols] = jnp.sum(
                d_conv * delayed(values, taps - 1 - k), axis=0, keepdims=True
            )
            if k < taps - 1:
                d_mix = d_mix + advanced(d_conv, taps - 1 - k) * conv_w[k : k + 1, cols]
        message[:seq, at : at + state] = d_mix.astype(bf16)
    message[:seq, 2 * state : 2 * state + heads] = d_step.astype(bf16)
    per_row = (inner + 2 * state) // wide
    packed = [
        g_conv[k : k + 1, i * wide : (i + 1) * wide] for k in range(taps + 1) for i in range(per_row)
    ]
    packed = packed + [jnp.zeros_like(packed[0])] * (TERM_ROWS - len(packed))
    message[seq:, :] = jnp.concatenate(packed).astype(bf16)


def cost(micros):
    return pl.CostEstimate(flops=int(micros * 1e9), transcendentals=0, bytes_accessed=0)


def pinned(shape, dtype):
    return pltpu.VMEM(shape, dtype)


def in_vmem(values):
    return [pltpu.with_memory_space_constraint(v, pltpu.VMEM) for v in values]


def student_forward(chips, levels, meta, inputs, loads):
    x, *_, w_x, _, conv_w, dt_bias, _, _, _ = inputs
    seq, width = x.shape
    inner, heads = w_x.shape[1], dt_bias.shape[1]
    both = conv_w.shape[1]
    f32, bf16 = jnp.float32, jnp.bfloat16
    wide = (inner + width) // chips
    shapes = [((seq, wide), bf16)] * chips + [
        ((seq, loads[0].shape[1]), f32),
        ((seq, both), f32), ((seq, both), f32), ((seq, inner), f32), ((seq, inner), f32),
        ((seq, inner), f32), ((seq, 128), f32), ((heads, seq, seq), f32), ((seq, seq), f32),
        ((seq, both - inner), f32), ((seq, heads), f32), ((seq, heads), f32),
    ]
    return pl.pallas_call(
        lambda *refs: forward_kernel(chips, levels, *refs),
        name="student_forward",
        in_specs=[SMEM] + [pl.BlockSpec(memory_space=pltpu.HBM)] * (INPUTS + LOADS),
        out_specs=[VMEM] * (LOADS + len(shapes)),
        out_shape=[pinned(v.shape, v.dtype) for v in loads]
        + [jax.ShapeDtypeStruct(s, t) for s, t in shapes[:chips]]
        + [pinned(s, t) for s, t in shapes[chips:]],
        scratch_shapes=[
            pltpu.VMEM((seq, width), bf16), pltpu.VMEM((seq, inner), bf16),
            pltpu.VMEM((chips, seq, wide), bf16), *[pltpu.VMEM(v.shape, v.dtype) for v in inputs],
            pltpu.SemaphoreType.DMA((INPUTS + LOADS,)),
        ],
        compiler_params=pltpu.CompilerParams(vmem_limit_bytes=15 << 20),
        cost_estimate=cost(6),
    )(meta, *[pltpu.with_memory_space_constraint(v, pltpu.HBM) for v in (*inputs, *loads)])


def student_backward(d_out, w_out, n_gain, conv_w, a_log, d_skip, saved):
    seq = d_out.shape[0]
    inner, heads = w_out.shape[0], a_log.shape[1]
    both = conv_w.shape[1]
    f32 = jnp.float32
    wide = both // TERM_CHUNKS
    return pl.pallas_call(
        backward_kernel,
        name="student_backward",
        in_specs=[VMEM] * (6 + len(saved)),
        out_specs=VMEM,
        out_shape=jax.ShapeDtypeStruct((seq + TERM_ROWS, wide), jnp.bfloat16),
        scratch_shapes=[
            pltpu.VMEM((8, both), f32), pltpu.VMEM((seq, inner), f32), pltpu.VMEM((seq, inner), f32),
        ],
        compiler_params=pltpu.CompilerParams(vmem_limit_bytes=8 << 20),
        cost_estimate=cost(9),
    )(d_out, *in_vmem([w_out]), n_gain, conv_w, a_log, d_skip, *in_vmem(saved))


def contract_kernel(count, lanes, extra, meta, *refs):
    cols, blocks = refs[:count], refs[count : 2 * count]
    mine, theirs, part = refs[2 * count :]
    f32 = jnp.float32
    seq = cols[0].shape[0]
    part[...] = lax.dot_general(
        jnp.concatenate([c[:, lanes] for c in cols]),
        jnp.concatenate([b[:seq, :] for b in blocks]),
        (((0,), (0,)), ((), ())),
        preferred_element_type=f32,
    ).reshape(part.shape)
    rows = part.shape[0] * part.shape[2]
    width = part.shape[3]
    mine[:rows, :] = part[:, pl.ds(meta[CORE], 1), :, :].reshape(rows, width)
    theirs[:rows, :] = part[:, pl.ds(1 - meta[CORE], 1), :, :].reshape(rows, width).astype(theirs.dtype)
    if extra:
        total = blocks[0][seq:, :].astype(f32)
        for block in blocks[1:]:
            total = total + block[seq:, :].astype(f32)
        mine[rows:, :] = total
        theirs[rows:, :] = total.astype(theirs.dtype)


def contract(meta, cols, lanes, blocks, levels):
    count = len(cols)
    width = blocks[0].shape[1]
    extra = blocks[0].shape[0] - cols[0].shape[0]
    own = (lanes.stop - lanes.start) // (2 * levels)
    rows = levels * own + extra
    return pl.pallas_call(
        lambda *refs: contract_kernel(count, lanes, extra, *refs),
        name="contract",
        in_specs=[SMEM] + [VMEM] * (2 * count),
        out_specs=[VMEM, VMEM],
        out_shape=[
            jax.ShapeDtypeStruct((rows, width), jnp.float32),
            jax.ShapeDtypeStruct((rows, width), jnp.bfloat16),
        ],
        scratch_shapes=[pltpu.VMEM((levels, 2, own, width), jnp.float32)],
        compiler_params=pltpu.CompilerParams(vmem_limit_bytes=6 << 20),
        cost_estimate=cost(0),
    )(meta, *cols, *blocks)


def share_kernel(levels, extra, meta, mine, got, own, *sent):
    rows = (mine.shape[0] - extra) // levels
    for k, to in ((0, own), *((i + 1, m) for i, m in enumerate(sent))):
        at = pl.multiple_of((meta[LEVEL] ^ k) * rows, rows)
        total = mine[pl.ds(at, rows), :] + got[pl.ds(at, rows), :].astype(jnp.float32)
        to[:rows, :] = total.astype(to.dtype)
        if extra:
            tail = slice(mine.shape[0] - extra, mine.shape[0])
            to[rows:, :] = (mine[tail, :] + got[tail, :].astype(jnp.float32)).astype(to.dtype)


def share(meta, mine, got, levels, extra):
    rows = (mine.shape[0] - extra) // levels + extra
    width = mine.shape[1]
    return pl.pallas_call(
        lambda *refs: share_kernel(levels, extra, *refs),
        name="share",
        in_specs=[SMEM, VMEM, VMEM],
        out_specs=[VMEM] * levels,
        out_shape=[jax.ShapeDtypeStruct((rows, width), jnp.float32)]
        + [jax.ShapeDtypeStruct((rows, width), jnp.bfloat16)] * (levels - 1),
        compiler_params=pltpu.CompilerParams(vmem_limit_bytes=3 << 20),
        cost_estimate=cost(0),
    )(meta, mine, got)


def finish_kernel(count, taps, meta, own_a, own_b, *refs):
    got_a, got_b = refs[:count], refs[count : 2 * count]
    g_bcdt, g_conv, g_gain, g_out, terms = refs[2 * count :]
    f32 = jnp.float32
    total = own_a[...]
    for part in got_a:
        total = total + part[...].astype(f32)
    g_out[...] = total
    total = own_b[...]
    for part in got_b:
        total = total + part[...].astype(f32)
    rows, wide = g_bcdt.shape[0], total.shape[1]
    g_bcdt[...] = total[:rows, : g_bcdt.shape[1]]
    terms[...] = total[rows:, :]
    lane = lax.broadcasted_iota(jnp.int32, (1, wide), 1)

    def window(first, width):
        start = meta[DEVICE] * width
        chunk = start // wide
        offset = start - chunk * wide
        left = pltpu.roll(terms[pl.ds(first + chunk, 1), :], wide - offset, 1)
        right = pltpu.roll(terms[pl.ds(first + chunk + 1, 1), :], wide - offset, 1)
        return jnp.where(lane < wide - offset, left, right)[:, :width]

    g_conv[...] = jnp.concatenate(
        [window(k * TERM_CHUNKS, g_conv.shape[1]) for k in range(taps)]
    )
    g_gain[...] = window(taps * TERM_CHUNKS, g_gain.shape[1])


def finish(meta, own_a, own_b, got_a, got_b, shapes):
    f32 = jnp.float32
    return pl.pallas_call(
        lambda *refs: finish_kernel(len(got_a), shapes[1][0], *refs),
        name="finish",
        in_specs=[SMEM] + [VMEM] * (2 + len(got_a) + len(got_b)),
        out_specs=[VMEM] * 4,
        out_shape=[jax.ShapeDtypeStruct(s, f32) for s in shapes],
        scratch_shapes=[pltpu.VMEM((TERM_ROWS, own_b.shape[1]), f32)],
        compiler_params=pltpu.CompilerParams(vmem_limit_bytes=3 << 20),
        cost_estimate=cost(0),
    )(meta, own_a, own_b, *got_a, *got_b)


def swap(values):
    size = lax.axis_size("head")
    return lax.ppermute(values, "head", [(i, i ^ 1) for i in range(size)])


def hop(values, step):
    size = lax.axis_size("head")
    return lax.ppermute(values, "head", [(i, i ^ (2 * step)) for i in range(size)])


def level(values, step):
    size = lax.axis_size("series")
    return lax.ppermute(values, "series", [(i, i ^ step) for i in range(size)])


def teacher_kernel(count, meta, *refs):
    pieces = refs[:count]
    gain, w_gate, w_up, readout, proj, mine, theirs, normed, acc = refs[count:]
    f32 = jnp.float32
    feat = proj.shape[0]
    feat_at = pl.multiple_of(meta[HEAD] * feat, feat)
    strip = 16
    start = 0
    for piece in pieces:
        for at in range(0, piece.shape[0], strip):
            values = piece[at : at + strip, :].astype(f32)
            mean_sq = jnp.mean(values * values, axis=-1, keepdims=True)
            scaled = values * lax.rsqrt(mean_sq + EPS) * gain[...]
            normed[start + at : start + at + strip, :] = scaled.astype(jnp.bfloat16)
        acc[start : start + piece.shape[0], :] = jnp.dot(
            piece[:, pl.ds(feat_at, feat)], proj[...], preferred_element_type=f32
        )
        start += piece.shape[0]
    tile = min(256, w_gate.shape[1])
    for at in range(0, w_gate.shape[1], tile):
        cols = slice(at, at + tile)
        gate = jnp.dot(normed[...], w_gate[:, cols], preferred_element_type=f32)
        upward = jnp.dot(normed[...], w_up[:, cols], preferred_element_type=f32)
        hidden = (gate / (1.0 + jnp.exp(-gate)) * upward).astype(jnp.bfloat16)
        acc[...] += jnp.dot(hidden, readout[cols, :], preferred_element_type=f32)
    rows = mine.shape[0]
    mine[...] = acc[:rows, :]
    theirs[...] = acc[rows:, :].astype(jnp.bfloat16)


def teacher_terms(meta, own, other, teacher_gain, w_gate, w_up, readout, proj):
    pieces = own + other
    rows = sum(p.shape[0] for p in own)
    width, out = w_gate.shape[0], readout.shape[1]
    return pl.pallas_call(
        lambda *refs: teacher_kernel(len(pieces), *refs),
        name="teacher",
        in_specs=[SMEM] + [VMEM] * (len(pieces) + 5),
        out_specs=[VMEM, VMEM],
        out_shape=[
            jax.ShapeDtypeStruct((rows, out), jnp.float32),
            jax.ShapeDtypeStruct((rows, out), jnp.bfloat16),
        ],
        scratch_shapes=[
            pltpu.VMEM((2 * rows, width), jnp.bfloat16),
            pltpu.VMEM((2 * rows, out), jnp.float32),
        ],
        compiler_params=pltpu.CompilerParams(vmem_limit_bytes=(5 << 20) + 2 * rows * (2 * width + 6 * out)),
        cost_estimate=cost(rows / 32),
    )(meta, *pieces, teacher_gain.reshape(1, width), *in_vmem([w_gate, w_up, readout, proj]))


def per_device(
    teacher_in, teacher_gain, w_gate, w_up, readout, distill_proj, building_ids, student_in,
    embed_rows, covariates, cov_proj, student_gain, w_x, w_bcdt, conv_w, dt_bias, a_log, d_skip,
    norm_gain, w_out,
):
    heads, levels = lax.axis_size("head"), lax.axis_size("series")
    chips = heads // 2
    head, z = lax.axis_index("head"), lax.axis_index("series")
    chip, core = head // 2, head % 2
    seq_len = teacher_in.shape[1]
    series_total = teacher_in.shape[0] * heads * levels
    bf16, f32 = jnp.bfloat16, jnp.float32

    own_rows = teacher_in[0]
    across = [hop(own_rows, k) for k in ((1, 2) if chips == 4 else range(1, chips))]
    meta = jnp.stack([head, core, z, chip, z * heads + head]).astype(jnp.int32)
    emb = lax.dynamic_slice_in_dim(embed_rows, building_ids[0], 1, 0)
    cov = lax.dynamic_slice_in_dim(covariates, building_ids[0], 1, 0)
    meta, emb, cov, w_gate = lax.optimization_barrier((meta, emb, cov, w_gate))
    row = [v.reshape(1, -1) for v in (student_gain, dt_bias, a_log, d_skip, norm_gain)]
    fwd = student_forward(
        chips, levels, meta,
        [
            student_in[0], emb, cov, cov_proj, row[0], w_x, w_bcdt.T, conv_w, row[1], row[2], row[3], row[4],
        ],
        [w_out, w_gate, w_up, readout, distill_proj],
    )
    w_out, w_gate, w_up, readout, distill_proj = fwd[:LOADS]
    fwd = fwd[LOADS:]
    cols, output, saved = list(fwd[:chips]), fwd[chips], fwd[chips + 1 :]
    def teach(own):
        return teacher_terms(
            meta, own, [swap(p) for p in own], teacher_gain, w_gate, w_up, readout, distill_proj
        )

    first = teach([own_rows])
    across, first, cols = lax.optimization_barrier((across, first, cols))

    def settle(terms, steps):
        mine, theirs = terms
        both = mine + swap(theirs).astype(f32)
        blocks = [both[i * seq_len : (i + 1) * seq_len] for i in range(len(steps))]
        return [hop(v.astype(bf16), k) if k else v for v, k in zip(blocks, steps)]

    def exchanged():
        return [cols[0]] + [hop(cols[k], k) for k in range(1, chips)]

    if chips == 4:
        half = seq_len // 2
        corner = [hop(across[1][:half], 1), hop(across[0][half:], 2)]
        second = teach(across)
        corner, second, cols = lax.optimization_barrier((corner, second, cols))
        parts = settle(first, (0,)) + settle(second, (1, 2))
        third = teach(corner)
        cols = exchanged()
        third, cols = lax.optimization_barrier((third, cols))
        parts = parts + settle(third, (3,))
    else:
        cols = exchanged()
        parts = settle(first, (0,))
        for k, v in enumerate(across):
            parts = parts + settle(teach([v]), (k + 1,))
    parts, cols = lax.optimization_barrier((parts, cols))
    target = parts[0]
    for part in parts[1:]:
        target = target + part.astype(f32)
    split = w_x.shape[1] // chips

    d_output = ((output - target) / series_total).astype(bf16)
    d_blocks = [d_output] + [hop(d_output, k) for k in range(1, chips)]
    message = student_backward(d_output, w_out, row[4], conv_w, row[2], row[3], saved)
    d_blocks, message = lax.optimization_barrier((d_blocks, message))

    messages = [message] + [hop(message, k) for k in range(1, chips)]
    mine, theirs = contract(meta, cols, slice(0, split), d_blocks, levels)
    own_a, *sent_a = share(meta, mine, swap(theirs), levels, 0)
    got_a = [level(v, k + 1) for k, v in enumerate(sent_a)]
    mine, theirs = contract(meta, cols, slice(split, cols[0].shape[1]), messages, levels)
    own_b, *sent_b = share(meta, mine, swap(theirs), levels, TERM_ROWS)
    got_a, sent_b = lax.optimization_barrier((got_a, sent_b))
    got_b = [level(v, k + 1) for k, v in enumerate(sent_b)]

    devices = heads * levels
    g_bcdt, g_conv, g_gain, g_out = finish(
        meta, own_a, own_b, got_a, got_b,
        [
            (w_bcdt.shape[0] // devices, w_bcdt.shape[1]), (conv_w.shape[0], conv_w.shape[1] // devices),
            (1, norm_gain.shape[0] // devices), (w_out.shape[0] // devices, w_out.shape[1]),
        ],
    )
    return (g_bcdt, g_conv, g_gain.reshape(-1), g_out)


def solution(mesh):
    return jax.shard_map(
        per_device,
        mesh=mesh,
        in_specs=(
            P(("series", "head"), None, None),
            P(),
            P(None, "head"),
            P(None, "head"),
            P("head", None),
            P("head", None),
            P(("series", "head")),
            P(("series", "head"), None, None),
            P(),
            P(),
            P(),
            P(),
            P(),
            P(),
            P(),
            P(),
            P(),
            P(),
            P(),
            P(),
        ),
        out_specs=(
            P(("series", "head"), None),
            P(None, ("series", "head")),
            P(("series", "head")),
            P(("series", "head"), None),
        ),
        check_vma=False,
    )
```

```python
import jax
import jax.numpy as jnp
from jax import lax
from jax.experimental import pallas as pl
from jax.experimental.pallas import tpu as pltpu
from jax.sharding import PartitionSpec as P

EPS = 1e-05


VMEM = pl.BlockSpec(memory_space=pltpu.VMEM)
SMEM = pl.BlockSpec(memory_space=pltpu.SMEM)
PAIR = 128
TERM_ROWS = 32
TERM_CHUNKS = 6
LOADS, INPUTS = 5, 12
NO_COST = pl.CostEstimate(flops=0, transcendentals=0, bytes_accessed=0)
HEAD, CORE, LEVEL, CHIP, DEVICE = range(5)


def exact_dot(left, right, dims=((1,), (0,))):
    return lax.dot_general(
        left, right, (dims, ((), ())), precision=lax.Precision.HIGHEST,
        preferred_element_type=jnp.float32,
    )


def halves(values):
    high = values.astype(jnp.bfloat16)
    return high, (values - high.astype(jnp.float32)).astype(jnp.bfloat16)


def close_dot(left, right, dims=((1,), (0,))):
    (lh, ll), (rh, rl) = halves(left), halves(right)

    def dot(a, b):
        return lax.dot_general(a, b, (dims, ((), ())), preferred_element_type=jnp.float32)

    return dot(lh, rh) + (dot(lh, rl) + dot(ll, rh))


def delayed(values, rows):
    if rows == 0:
        return values
    at = lax.broadcasted_iota(jnp.int32, values.shape, 0)
    return jnp.where(at >= rows, pltpu.roll(values, rows, 0), 0.0)


def advanced(values, rows):
    if rows == 0:
        return values
    size = values.shape[0]
    at = lax.broadcasted_iota(jnp.int32, values.shape, 0)
    return jnp.where(at < size - rows, pltpu.roll(values, size - rows, 0), 0.0)


def head_lanes(head_count, width):
    head = lax.broadcasted_iota(jnp.int32, (head_count, width), 0)
    lane = lax.broadcasted_iota(jnp.int32, (head_count, width), 1)
    size = width // head_count
    return ((lane >= head * size) & (lane < (head + 1) * size)).astype(jnp.float32)


def stacked_by_head(values, head_size):
    lane = lax.broadcasted_iota(jnp.int32, values.shape, 1)
    return jnp.concatenate(
        [
            jnp.where((lane >= at) & (lane < at + head_size), values, 0.0)
            for at in range(0, values.shape[1], head_size)
        ]
    )


def forward_kernel(
    chips, levels, meta, *refs
):
    far, refs = refs[: INPUTS + LOADS], refs[INPUTS + LOADS :]
    near, refs = list(refs[:LOADS]), refs[LOADS:]
    held, sems, refs = list(refs[-INPUTS - 1 : -1]), refs[-1], refs[: -INPUTS - 1]
    loads = [pltpu.make_async_copy(f, n, sems.at[i]) for i, (f, n) in enumerate(zip(far, held + near))]
    for copy in loads[:INPUTS]:
        copy.start()
    for copy in loads[:INPUTS]:
        copy.wait()
    loads = loads[INPUTS:]
    for copy in loads:
        copy.start()
    x, emb, cov, cov_proj, s_gain, w_x, w_bcdt, conv_w, dt_bias, a_log, d_skip, n_gain = held
    w_out = near[0]
    outgoing = refs[:chips]
    (output, mix, slope, xa, dt_wide, y, inv, decay_t, scores_t, bc, dt, gate_dt,
     normed, rounded, sorted_cols) = refs[chips:]
    f32 = jnp.float32
    seq, inner = xa.shape
    heads = dt.shape[1]
    state = bc.shape[1] // 2
    head_size = inner // heads
    extra = emb[...].astype(f32) + jnp.dot(cov[...], cov_proj[...], preferred_element_type=f32)[:1]
    base = x[...].astype(f32) + extra
    mean_sq = jnp.mean(base * base, axis=-1, keepdims=True)
    normed[...] = (base * lax.rsqrt(mean_sq + EPS) * s_gain[...]).astype(jnp.bfloat16)
    projected = lax.dot_general(
        normed[...], w_bcdt[...], (((1,), (1,)), ((), ())), preferred_element_type=f32
    )
    mix[:, :inner] = jnp.dot(normed[...], w_x[...], preferred_element_type=f32)
    mix[:, inner:] = projected[:, : 2 * state]

    taps = conv_w.shape[0]
    for at in range(0, inner + 2 * state, 256):
        cols = slice(at, at + 256)
        values = mix[:, cols]
        conv = values * conv_w[taps - 1 : taps, cols]
        for k in range(taps - 1):
            conv = conv + delayed(values, taps - 1 - k) * conv_w[k : k + 1, cols]
        gate = 1.0 / (1.0 + jnp.exp(-conv))
        slope[:, cols] = gate * (1.0 + conv * (1.0 - gate))
        if at < inner:
            xa[:, cols] = conv * gate
        else:
            bc[:, at - inner : at - inner + 256] = conv * gate

    logits = projected[:, 2 * state : 2 * state + heads] + dt_bias[...]
    steps = jnp.maximum(logits, 0.0) + jnp.log1p(jnp.exp(-jnp.abs(logits)))
    dt[...] = steps
    gate_dt[...] = 1.0 / (1.0 + jnp.exp(-logits))
    row = lax.broadcasted_iota(jnp.int32, (seq, seq), 0)
    col = lax.broadcasted_iota(jnp.int32, (seq, seq), 1)
    running = exact_dot((row >= col).astype(f32), steps * -jnp.exp(a_log[...]))
    running_t = jnp.concatenate([running, jnp.zeros((seq, 128 - heads), f32)], axis=1).T
    lanes = head_lanes(heads, inner)
    dt_wide[...] = exact_dot(steps, lanes)
    scores = exact_dot(bc[:, state:], bc[:, :state], ((1,), (1,)))
    scores_t[...] = scores.T

    group = PAIR // head_size
    for p in range(inner // PAIR):
        cols = slice(p * PAIR, (p + 1) * PAIR)
        weights = []
        for h in range(p * group, (p + 1) * group):
            down, across = running[:, h : h + 1], running_t[h : h + 1, :]
            decay = jnp.exp(jnp.where(row >= col, down - across, -1e30))
            decay_t[h] = jnp.exp(jnp.where(col >= row, across - down, -1e30))
            weights.append(scores * decay)
        held = stacked_by_head(dt_wide[:, cols] * xa[:, cols], head_size)
        y[:, cols] = close_dot(jnp.concatenate(weights, axis=1), held)

    skip = exact_dot(jnp.broadcast_to(d_skip[...], (8, heads)), lanes)[:1]
    mixed = y[...] + skip * xa[...]
    scale = lax.rsqrt(jnp.mean(mixed * mixed, axis=-1, keepdims=True) + EPS)
    inv[...] = jnp.broadcast_to(scale, inv.shape)
    rounded[...] = (mixed * scale * n_gain[...]).astype(jnp.bfloat16)
    loads[0].wait()
    output[...] = jnp.dot(rounded[...], w_out[...], preferred_element_type=f32)

    start = 0
    for values in (rounded, normed):
        width = values.shape[1] // (levels * chips)
        for z in range(levels):
            for chip in range(chips):
                at = (z * chips + chip) * width
                sorted_cols[chip, :, start : start + width] = values[:, at : at + width]
            start += width
    for k in range(chips):
        outgoing[k][...] = sorted_cols[meta[CHIP] ^ k]
    for copy in loads[1:]:
        copy.wait()


def backward_kernel(
    d_out, w_out, n_gain, conv_w, a_log, d_skip, mix, slope, xa, dt_wide, y, inv, decay_t, scores_t,
    bc, dt, gate_dt, message, g_conv, d_mixed, through,
):
    f32 = jnp.float32
    seq, inner = xa.shape
    heads = dt.shape[1]
    state = bc.shape[1] // 2
    head_size = inner // heads
    taps = conv_w.shape[0]
    lanes = head_lanes(heads, inner)
    skip = exact_dot(jnp.broadcast_to(d_skip[...], (8, heads)), lanes)[:1]
    scale = inv[:, :1]
    d_norm = lax.dot_general(
        d_out[...], w_out[...], (((1,), (1,)), ((), ())), preferred_element_type=f32
    )
    unit = (y[...] + skip * xa[...]) * scale
    wide = message.shape[1]
    bf16 = jnp.bfloat16
    message[...] = jnp.zeros_like(message)
    g_conv[...] = jnp.zeros_like(g_conv)
    g_conv[taps : taps + 1, :inner] = jnp.sum(d_norm * unit, axis=0, keepdims=True)
    pulled = d_norm * n_gain[...]
    d_mixed[...] = scale * (pulled - unit * jnp.mean(pulled * unit, axis=-1, keepdims=True))

    group = PAIR // head_size
    d_scores_t = jnp.zeros((seq, seq), f32)
    scored = scores_t[...]
    for p in range(inner // PAIR):
        cols = slice(p * PAIR, (p + 1) * PAIR)
        got = d_mixed[:, cols]
        held = dt_wide[:, cols] * xa[:, cols]
        weights = jnp.concatenate(
            [scored * decay_t[h] for h in range(p * group, (p + 1) * group)], axis=1
        )
        through[:, cols] = close_dot(weights, stacked_by_head(got, head_size))
        outer = close_dot(stacked_by_head(held, head_size), got, ((1,), (1,)))
        for i in range(group):
            d_scores_t = d_scores_t + outer[i * seq : (i + 1) * seq] * decay_t[p * group + i]

    d_dt = exact_dot(through[...] * xa[...], lanes, ((1,), (1,)))
    d_running = exact_dot(d_mixed[...] * y[...], lanes, ((1,), (1,))) - dt[...] * d_dt
    row = lax.broadcasted_iota(jnp.int32, (seq, seq), 0)
    col = lax.broadcasted_iota(jnp.int32, (seq, seq), 1)
    later = exact_dot((col >= row).astype(f32), d_running)
    d_step = (d_dt + later * -jnp.exp(a_log[...])) * gate_dt[...]

    for at in range(0, inner, 256):
        cols = slice(at, at + 256)
        d_act = dt_wide[:, cols] * through[:, cols] + skip[:, cols] * d_mixed[:, cols]
        d_conv = d_act * slope[:, cols]
        values = mix[:, cols]
        for k in range(taps):
            g_conv[k : k + 1, cols] = jnp.sum(
                d_conv * delayed(values, taps - 1 - k), axis=0, keepdims=True
            )
    d_b = exact_dot(d_scores_t, bc[:, state:])
    d_c = exact_dot(d_scores_t.T, bc[:, :state])
    for at, d_act in ((0, d_b), (state, d_c)):
        cols = slice(inner + at, inner + at + state)
        d_conv = d_act * slope[:, cols]
        values = mix[:, cols]
        d_mix = d_conv * conv_w[taps - 1 : taps, cols]
        for k in range(taps):
            g_conv[k : k + 1, cols] = jnp.sum(
                d_conv * delayed(values, taps - 1 - k), axis=0, keepdims=True
            )
            if k < taps - 1:
                d_mix = d_mix + advanced(d_conv, taps - 1 - k) * conv_w[k : k + 1, cols]
        message[:seq, at : at + state] = d_mix.astype(bf16)
    message[:seq, 2 * state : 2 * state + heads] = d_step.astype(bf16)
    per_row = (inner + 2 * state) // wide
    packed = [
        g_conv[k : k + 1, i * wide : (i + 1) * wide] for k in range(taps + 1) for i in range(per_row)
    ]
    packed = packed + [jnp.zeros_like(packed[0])] * (TERM_ROWS - len(packed))
    message[seq:, :] = jnp.concatenate(packed).astype(bf16)


def pinned(shape, dtype):
    return pltpu.VMEM(shape, dtype)


def in_vmem(values):
    return [pltpu.with_memory_space_constraint(v, pltpu.VMEM) for v in values]


def student_forward(chips, levels, meta, inputs, loads):
    x, *_, w_x, _, conv_w, dt_bias, _, _, _ = inputs
    seq, width = x.shape
    inner, heads = w_x.shape[1], dt_bias.shape[1]
    both = conv_w.shape[1]
    f32, bf16 = jnp.float32, jnp.bfloat16
    wide = (inner + width) // chips
    shapes = [((seq, wide), bf16)] * chips + [
        ((seq, loads[0].shape[1]), f32),
        ((seq, both), f32), ((seq, both), f32), ((seq, inner), f32), ((seq, inner), f32),
        ((seq, inner), f32), ((seq, 128), f32), ((heads, seq, seq), f32), ((seq, seq), f32),
        ((seq, both - inner), f32), ((seq, heads), f32), ((seq, heads), f32),
    ]
    return pl.pallas_call(
        lambda *refs: forward_kernel(chips, levels, *refs),
        name="student_forward",
        in_specs=[SMEM] + [pl.BlockSpec(memory_space=pltpu.HBM)] * (INPUTS + LOADS),
        out_specs=[VMEM] * (LOADS + len(shapes)),
        out_shape=[pinned(v.shape, v.dtype) for v in loads]
        + [jax.ShapeDtypeStruct(s, t) for s, t in shapes[:chips]]
        + [pinned(s, t) for s, t in shapes[chips:]],
        scratch_shapes=[
            pltpu.VMEM((seq, width), bf16), pltpu.VMEM((seq, inner), bf16),
            pltpu.VMEM((chips, seq, wide), bf16), *[pltpu.VMEM(v.shape, v.dtype) for v in inputs],
            pltpu.SemaphoreType.DMA((INPUTS + LOADS,)),
        ],
        compiler_params=pltpu.CompilerParams(vmem_limit_bytes=15 << 20),
        cost_estimate=NO_COST,
    )(meta, *[pltpu.with_memory_space_constraint(v, pltpu.HBM) for v in (*inputs, *loads)])


def student_backward(d_out, w_out, n_gain, conv_w, a_log, d_skip, saved):
    seq = d_out.shape[0]
    inner, heads = w_out.shape[0], a_log.shape[1]
    both = conv_w.shape[1]
    f32 = jnp.float32
    wide = both // TERM_CHUNKS
    return pl.pallas_call(
        backward_kernel,
        name="student_backward",
        in_specs=[VMEM] * (6 + len(saved)),
        out_specs=VMEM,
        out_shape=jax.ShapeDtypeStruct((seq + TERM_ROWS, wide), jnp.bfloat16),
        scratch_shapes=[
            pltpu.VMEM((8, both), f32), pltpu.VMEM((seq, inner), f32), pltpu.VMEM((seq, inner), f32),
        ],
        compiler_params=pltpu.CompilerParams(vmem_limit_bytes=8 << 20),
        cost_estimate=NO_COST,
    )(d_out, *in_vmem([w_out]), n_gain, conv_w, a_log, d_skip, *in_vmem(saved))


def contract_kernel(count, lanes, extra, meta, *refs):
    cols, blocks = refs[:count], refs[count : 2 * count]
    mine, theirs, part = refs[2 * count :]
    f32 = jnp.float32
    seq = cols[0].shape[0]
    part[...] = lax.dot_general(
        jnp.concatenate([c[:, lanes] for c in cols]),
        jnp.concatenate([b[:seq, :] for b in blocks]),
        (((0,), (0,)), ((), ())),
        preferred_element_type=f32,
    ).reshape(part.shape)
    rows = part.shape[0] * part.shape[2]
    width = part.shape[3]
    mine[:rows, :] = part[:, pl.ds(meta[CORE], 1), :, :].reshape(rows, width)
    theirs[:rows, :] = part[:, pl.ds(1 - meta[CORE], 1), :, :].reshape(rows, width).astype(theirs.dtype)
    if extra:
        total = blocks[0][seq:, :].astype(f32)
        for block in blocks[1:]:
            total = total + block[seq:, :].astype(f32)
        mine[rows:, :] = total
        theirs[rows:, :] = total.astype(theirs.dtype)


def contract(meta, cols, lanes, blocks, levels):
    count = len(cols)
    width = blocks[0].shape[1]
    extra = blocks[0].shape[0] - cols[0].shape[0]
    own = (lanes.stop - lanes.start) // (2 * levels)
    rows = levels * own + extra
    return pl.pallas_call(
        lambda *refs: contract_kernel(count, lanes, extra, *refs),
        name="contract",
        in_specs=[SMEM] + [VMEM] * (2 * count),
        out_specs=[VMEM, VMEM],
        out_shape=[
            jax.ShapeDtypeStruct((rows, width), jnp.float32),
            jax.ShapeDtypeStruct((rows, width), jnp.bfloat16),
        ],
        scratch_shapes=[pltpu.VMEM((levels, 2, own, width), jnp.float32)],
        compiler_params=pltpu.CompilerParams(vmem_limit_bytes=6 << 20),
        cost_estimate=NO_COST,
    )(meta, *cols, *blocks)


def share_kernel(levels, extra, meta, mine_a, got_a, mine_b, got_b, own_a, own_b, *sent):
    f32 = jnp.float32

    def chip_sum(mine, got, at, rows):
        return mine[pl.ds(at, rows), :] + got[pl.ds(at, rows), :].astype(f32)

    rows_a = mine_a.shape[0] // levels
    rows_b = (mine_b.shape[0] - extra) // levels
    width = mine_a.shape[1]
    tail = chip_sum(mine_b, got_b, levels * rows_b, extra)
    for k in range(levels):
        level_at = meta[LEVEL] ^ k
        part_a = chip_sum(mine_a, got_a, pl.multiple_of(level_at * rows_a, rows_a), rows_a)
        part_b = chip_sum(mine_b, got_b, pl.multiple_of(level_at * rows_b, rows_b), rows_b)
        if k == 0:
            own_a[...] = part_a
            own_b[:rows_b, :] = part_b
            own_b[rows_b:, :] = tail
        else:
            to = sent[k - 1]
            if rows_a != rows_b + extra:
                to[...] = jnp.zeros_like(to)
            to[:rows_a, :width] = part_a.astype(to.dtype)
            to[:rows_b, width:] = part_b.astype(to.dtype)
            to[rows_b : rows_b + extra, width:] = tail.astype(to.dtype)


def share(meta, a, b, levels, extra):
    rows_a = a[0].shape[0] // levels
    rows_b = (b[0].shape[0] - extra) // levels + extra
    width_a, width_b = a[0].shape[1], b[0].shape[1]
    f32 = jnp.float32
    return pl.pallas_call(
        lambda *refs: share_kernel(levels, extra, *refs),
        name="share",
        in_specs=[SMEM] + [VMEM] * 4,
        out_specs=[VMEM] * (levels + 1),
        out_shape=[
            jax.ShapeDtypeStruct((rows_a, width_a), f32), jax.ShapeDtypeStruct((rows_b, width_b), f32),
        ]
        + [jax.ShapeDtypeStruct((max(rows_a, rows_b), width_a + width_b), jnp.bfloat16)] * (levels - 1),
        compiler_params=pltpu.CompilerParams(vmem_limit_bytes=4 << 20),
        cost_estimate=NO_COST,
    )(meta, *a, *b)


def finish_kernel(count, taps, meta, own_a, own_b, *refs):
    got = refs[:count]
    g_bcdt, g_conv, g_gain, g_out, terms = refs[count:]
    f32 = jnp.float32
    total = own_a[...]
    rows, width = own_a.shape
    for part in got:
        total = total + part[:rows, :width].astype(f32)
    g_out[...] = total
    total = own_b[...]
    for part in got:
        total = total + part[: own_b.shape[0], width:].astype(f32)
    rows, wide = g_bcdt.shape[0], total.shape[1]
    g_bcdt[...] = total[:rows, : g_bcdt.shape[1]]
    terms[...] = total[rows:, :]
    lane = lax.broadcasted_iota(jnp.int32, (1, wide), 1)

    def window(first, width):
        start = meta[DEVICE] * width
        chunk = start // wide
        offset = start - chunk * wide
        left = pltpu.roll(terms[pl.ds(first + chunk, 1), :], wide - offset, 1)
        right = pltpu.roll(terms[pl.ds(first + chunk + 1, 1), :], wide - offset, 1)
        return jnp.where(lane < wide - offset, left, right)[:, :width]

    g_conv[...] = jnp.concatenate(
        [window(k * TERM_CHUNKS, g_conv.shape[1]) for k in range(taps)]
    )
    g_gain[...] = window(taps * TERM_CHUNKS, g_gain.shape[1])


def finish(meta, own_a, own_b, got, shapes):
    f32 = jnp.float32
    return pl.pallas_call(
        lambda *refs: finish_kernel(len(got), shapes[1][0], *refs),
        name="finish",
        in_specs=[SMEM] + [VMEM] * (2 + len(got)),
        out_specs=[VMEM] * 4,
        out_shape=[jax.ShapeDtypeStruct(s, f32) for s in shapes],
        scratch_shapes=[pltpu.VMEM((TERM_ROWS, own_b.shape[1]), f32)],
        compiler_params=pltpu.CompilerParams(vmem_limit_bytes=3 << 20),
        cost_estimate=NO_COST,
    )(meta, own_a, own_b, *got)


def swap(values):
    size = lax.axis_size("head")
    return lax.ppermute(values, "head", [(i, i ^ 1) for i in range(size)])


def hop(values, step):
    size = lax.axis_size("head")
    return lax.ppermute(values, "head", [(i, i ^ (2 * step)) for i in range(size)])


def level(values, step):
    size = lax.axis_size("series")
    return lax.ppermute(values, "series", [(i, i ^ step) for i in range(size)])


def teacher_kernel(count, meta, *refs):
    pieces = refs[:count]
    gain, w_gate, w_up, readout, proj, mine, theirs, normed, acc = refs[count:]
    f32 = jnp.float32
    feat = proj.shape[0]
    feat_at = pl.multiple_of(meta[HEAD] * feat, feat)
    strip = 16
    start = 0
    for piece in pieces:
        for at in range(0, piece.shape[0], strip):
            values = piece[at : at + strip, :].astype(f32)
            mean_sq = jnp.mean(values * values, axis=-1, keepdims=True)
            scaled = values * lax.rsqrt(mean_sq + EPS) * gain[...]
            normed[start + at : start + at + strip, :] = scaled.astype(jnp.bfloat16)
        acc[start : start + piece.shape[0], :] = jnp.dot(
            piece[:, pl.ds(feat_at, feat)], proj[...], preferred_element_type=f32
        )
        start += piece.shape[0]
    tile = min(256, w_gate.shape[1])
    for at in range(0, w_gate.shape[1], tile):
        cols = slice(at, at + tile)
        gate = jnp.dot(normed[...], w_gate[:, cols], preferred_element_type=f32)
        upward = jnp.dot(normed[...], w_up[:, cols], preferred_element_type=f32)
        hidden = (gate / (1.0 + jnp.exp(-gate)) * upward).astype(jnp.bfloat16)
        acc[...] += jnp.dot(hidden, readout[cols, :], preferred_element_type=f32)
    rows = mine.shape[0]
    mine[...] = acc[:rows, :]
    theirs[...] = acc[rows:, :].astype(jnp.bfloat16)


def teacher_terms(meta, own, other, teacher_gain, w_gate, w_up, readout, proj):
    pieces = own + other
    rows = sum(p.shape[0] for p in own)
    width, out = w_gate.shape[0], readout.shape[1]
    return pl.pallas_call(
        lambda *refs: teacher_kernel(len(pieces), *refs),
        name="teacher",
        in_specs=[SMEM] + [VMEM] * (len(pieces) + 5),
        out_specs=[VMEM, VMEM],
        out_shape=[
            jax.ShapeDtypeStruct((rows, out), jnp.float32),
            jax.ShapeDtypeStruct((rows, out), jnp.bfloat16),
        ],
        scratch_shapes=[
            pltpu.VMEM((2 * rows, width), jnp.bfloat16),
            pltpu.VMEM((2 * rows, out), jnp.float32),
        ],
        compiler_params=pltpu.CompilerParams(vmem_limit_bytes=(5 << 20) + 2 * rows * (2 * width + 6 * out)),
        cost_estimate=NO_COST,
    )(meta, *pieces, teacher_gain.reshape(1, width), *in_vmem([w_gate, w_up, readout, proj]))


def per_device(
    teacher_in, teacher_gain, w_gate, w_up, readout, distill_proj, building_ids, student_in,
    embed_rows, covariates, cov_proj, student_gain, w_x, w_bcdt, conv_w, dt_bias, a_log, d_skip,
    norm_gain, w_out,
):
    heads, levels = lax.axis_size("head"), lax.axis_size("series")
    chips = heads // 2
    head, z = lax.axis_index("head"), lax.axis_index("series")
    chip, core = head // 2, head % 2
    seq_len = teacher_in.shape[1]
    series_total = teacher_in.shape[0] * heads * levels
    bf16, f32 = jnp.bfloat16, jnp.float32

    own_rows = teacher_in[0]
    across = [hop(own_rows, k) for k in ((1, 2) if chips == 4 else range(1, chips))]
    meta = jnp.stack([head, core, z, chip, z * heads + head]).astype(jnp.int32)
    emb = lax.dynamic_slice_in_dim(embed_rows, building_ids[0], 1, 0)
    cov = lax.dynamic_slice_in_dim(covariates, building_ids[0], 1, 0)
    meta, emb, cov, w_gate = lax.optimization_barrier((meta, emb, cov, w_gate))
    row = [v.reshape(1, -1) for v in (student_gain, dt_bias, a_log, d_skip, norm_gain)]
    fwd = student_forward(
        chips, levels, meta,
        [
            student_in[0], emb, cov, cov_proj, row[0], w_x, w_bcdt.T, conv_w, row[1], row[2], row[3], row[4],
        ],
        [w_out, w_gate, w_up, readout, distill_proj],
    )
    w_out, w_gate, w_up, readout, distill_proj = fwd[:LOADS]
    fwd = fwd[LOADS:]
    cols, output, saved = list(fwd[:chips]), fwd[chips], fwd[chips + 1 :]
    def teach(own):
        return teacher_terms(
            meta, own, [swap(p) for p in own], teacher_gain, w_gate, w_up, readout, distill_proj
        )

    first = teach([own_rows])
    across, first, cols = lax.optimization_barrier((across, first, cols))

    def settle(terms, steps):
        mine, theirs = terms
        both = mine + swap(theirs).astype(f32)
        blocks = [both[i * seq_len : (i + 1) * seq_len] for i in range(len(steps))]
        return [hop(v.astype(bf16), k) if k else v for v, k in zip(blocks, steps)]

    def exchanged():
        return [cols[0]] + [hop(cols[k], k) for k in range(1, chips)]

    if chips == 4:
        half = seq_len // 2
        corner = [hop(across[1][:half], 1), hop(across[0][half:], 2)]
        second = teach(across)
        corner, second, cols = lax.optimization_barrier((corner, second, cols))
        parts = settle(first, (0,)) + settle(second, (1, 2))
        third = teach(corner)
        cols = exchanged()
        third, cols = lax.optimization_barrier((third, cols))
        parts = parts + settle(third, (3,))
    else:
        cols = exchanged()
        parts = settle(first, (0,))
        for k, v in enumerate(across):
            parts = parts + settle(teach([v]), (k + 1,))
    target = parts[0]
    for part in parts[1:]:
        target = target + part.astype(f32)
    split = w_x.shape[1] // chips

    d_output = ((output - target) / series_total).astype(bf16)
    d_blocks = [d_output] + [hop(d_output, k) for k in range(1, chips)]
    message = student_backward(d_output, w_out, row[4], conv_w, row[2], row[3], saved)
    message, d_blocks[1], cols = lax.optimization_barrier((message, d_blocks[1], cols))
    messages = [message] + [hop(message, k) for k in range(1, chips)]
    first_a, other_a = contract(meta, cols, slice(0, split), d_blocks, levels)
    messages, first_a, other_a = lax.optimization_barrier((messages, first_a, other_a))
    first_b, other_b = contract(meta, cols, slice(split, cols[0].shape[1]), messages, levels)
    own_a, own_b, *sent = share(
        meta, (first_a, swap(other_a)), (first_b, swap(other_b)), levels, TERM_ROWS
    )
    got = [level(v, k + 1) for k, v in enumerate(sent)]

    devices = heads * levels
    g_bcdt, g_conv, g_gain, g_out = finish(
        meta, own_a, own_b, got,
        [
            (w_bcdt.shape[0] // devices, w_bcdt.shape[1]), (conv_w.shape[0], conv_w.shape[1] // devices),
            (1, norm_gain.shape[0] // devices), (w_out.shape[0] // devices, w_out.shape[1]),
        ],
    )
    return (g_bcdt, g_conv, g_gain.reshape(-1), g_out)


def solution(mesh):
    return jax.shard_map(
        per_device,
        mesh=mesh,
        in_specs=(
            P(("series", "head"), None, None),
            P(),
            P(None, "head"),
            P(None, "head"),
            P("head", None),
            P("head", None),
            P(("series", "head")),
            P(("series", "head"), None, None),
            P(),
            P(),
            P(),
            P(),
            P(),
            P(),
            P(),
            P(),
            P(),
            P(),
            P(),
            P(),
        ),
        out_specs=(
            P(("series", "head"), None),
            P(None, ("series", "head")),
            P(("series", "head")),
            P(("series", "head"), None),
        ),
        check_vma=False,
    )
```

```python
import jax
import jax.numpy as jnp
from jax import lax
from jax.experimental import pallas as pl
from jax.experimental.pallas import tpu as pltpu
from jax.sharding import PartitionSpec as P

EPS = 1e-05


VMEM = pl.BlockSpec(memory_space=pltpu.VMEM)
SMEM = pl.BlockSpec(memory_space=pltpu.SMEM)
PAIR = 128
TERM_ROWS = 32
TERM_CHUNKS = 6
LOADS, INPUTS = 5, 12
NO_COST = pl.CostEstimate(flops=0, transcendentals=0, bytes_accessed=0)
HEAD, CORE, LEVEL, CHIP, DEVICE = range(5)


def exact_dot(left, right, dims=((1,), (0,))):
    return lax.dot_general(
        left, right, (dims, ((), ())), precision=lax.Precision.HIGHEST,
        preferred_element_type=jnp.float32,
    )


def halves(values):
    high = values.astype(jnp.bfloat16)
    return high, (values - high.astype(jnp.float32)).astype(jnp.bfloat16)


def close_dot(left, right, dims=((1,), (0,))):
    (lh, ll), (rh, rl) = halves(left), halves(right)

    def dot(a, b):
        return lax.dot_general(a, b, (dims, ((), ())), preferred_element_type=jnp.float32)

    return dot(lh, rh) + (dot(lh, rl) + dot(ll, rh))


def delayed(values, rows):
    if rows == 0:
        return values
    at = lax.broadcasted_iota(jnp.int32, values.shape, 0)
    return jnp.where(at >= rows, pltpu.roll(values, rows, 0), 0.0)


def advanced(values, rows):
    if rows == 0:
        return values
    size = values.shape[0]
    at = lax.broadcasted_iota(jnp.int32, values.shape, 0)
    return jnp.where(at < size - rows, pltpu.roll(values, size - rows, 0), 0.0)


def head_lanes(head_count, width):
    head = lax.broadcasted_iota(jnp.int32, (head_count, width), 0)
    lane = lax.broadcasted_iota(jnp.int32, (head_count, width), 1)
    size = width // head_count
    return ((lane >= head * size) & (lane < (head + 1) * size)).astype(jnp.float32)


def stacked_by_head(values, head_size):
    lane = lax.broadcasted_iota(jnp.int32, values.shape, 1)
    return jnp.concatenate(
        [
            jnp.where((lane >= at) & (lane < at + head_size), values, 0.0)
            for at in range(0, values.shape[1], head_size)
        ]
    )


def forward_kernel(
    chips, levels, meta, *refs
):
    far, refs = refs[: INPUTS + LOADS], refs[INPUTS + LOADS :]
    near, refs = list(refs[:LOADS]), refs[LOADS:]
    held, sems, refs = list(refs[-INPUTS - 1 : -1]), refs[-1], refs[: -INPUTS - 1]
    loads = [pltpu.make_async_copy(f, n, sems.at[i]) for i, (f, n) in enumerate(zip(far, held + near))]
    for copy in loads[:INPUTS]:
        copy.start()
    for copy in loads[:INPUTS]:
        copy.wait()
    loads = loads[INPUTS:]
    for copy in loads:
        copy.start()
    x, emb, cov, cov_proj, s_gain, w_x, w_bcdt, conv_w, dt_bias, a_log, d_skip, n_gain = held
    w_out = near[0]
    outgoing = refs[:chips]
    (output, mix, slope, xa, dt_wide, y, inv, decay_t, scores_t, bc, dt, gate_dt,
     normed, rounded, sorted_cols) = refs[chips:]
    f32 = jnp.float32
    seq, inner = xa.shape
    heads = dt.shape[1]
    state = bc.shape[1] // 2
    head_size = inner // heads
    extra = emb[...].astype(f32) + jnp.dot(cov[...], cov_proj[...], preferred_element_type=f32)[:1]
    base = x[...].astype(f32) + extra
    mean_sq = jnp.mean(base * base, axis=-1, keepdims=True)
    normed[...] = (base * lax.rsqrt(mean_sq + EPS) * s_gain[...]).astype(jnp.bfloat16)
    projected = lax.dot_general(
        normed[...], w_bcdt[...], (((1,), (1,)), ((), ())), preferred_element_type=f32
    )
    mix[:, :inner] = jnp.dot(normed[...], w_x[...], preferred_element_type=f32)
    mix[:, inner:] = projected[:, : 2 * state]

    taps = conv_w.shape[0]
    for at in range(0, inner + 2 * state, 256):
        cols = slice(at, at + 256)
        values = mix[:, cols]
        conv = values * conv_w[taps - 1 : taps, cols]
        for k in range(taps - 1):
            conv = conv + delayed(values, taps - 1 - k) * conv_w[k : k + 1, cols]
        gate = 1.0 / (1.0 + jnp.exp(-conv))
        slope[:, cols] = gate * (1.0 + conv * (1.0 - gate))
        if at < inner:
            xa[:, cols] = conv * gate
        else:
            bc[:, at - inner : at - inner + 256] = conv * gate

    logits = projected[:, 2 * state : 2 * state + heads] + dt_bias[...]
    steps = jnp.maximum(logits, 0.0) + jnp.log1p(jnp.exp(-jnp.abs(logits)))
    dt[...] = steps
    gate_dt[...] = 1.0 / (1.0 + jnp.exp(-logits))
    row = lax.broadcasted_iota(jnp.int32, (seq, seq), 0)
    col = lax.broadcasted_iota(jnp.int32, (seq, seq), 1)
    running = exact_dot((row >= col).astype(f32), steps * -jnp.exp(a_log[...]))
    running_t = jnp.concatenate([running, jnp.zeros((seq, 128 - heads), f32)], axis=1).T
    lanes = head_lanes(heads, inner)
    dt_wide[...] = exact_dot(steps, lanes)
    scores = exact_dot(bc[:, state:], bc[:, :state], ((1,), (1,)))
    scores_t[...] = scores.T

    group = PAIR // head_size
    for p in range(inner // PAIR):
        cols = slice(p * PAIR, (p + 1) * PAIR)
        weights = []
        for h in range(p * group, (p + 1) * group):
            down, across = running[:, h : h + 1], running_t[h : h + 1, :]
            decay = jnp.exp(jnp.where(row >= col, down - across, -1e30))
            decay_t[h] = jnp.exp(jnp.where(col >= row, across - down, -1e30))
            weights.append(scores * decay)
        held = stacked_by_head(dt_wide[:, cols] * xa[:, cols], head_size)
        y[:, cols] = close_dot(jnp.concatenate(weights, axis=1), held)

    skip = exact_dot(jnp.broadcast_to(d_skip[...], (8, heads)), lanes)[:1]
    mixed = y[...] + skip * xa[...]
    scale = lax.rsqrt(jnp.mean(mixed * mixed, axis=-1, keepdims=True) + EPS)
    inv[...] = jnp.broadcast_to(scale, inv.shape)
    rounded[...] = (mixed * scale * n_gain[...]).astype(jnp.bfloat16)
    loads[0].wait()
    output[...] = jnp.dot(rounded[...], w_out[...], preferred_element_type=f32)

    start = 0
    for values in (rounded, normed):
        width = values.shape[1] // (levels * chips)
        for z in range(levels):
            for chip in range(chips):
                at = (z * chips + chip) * width
                sorted_cols[chip, :, start : start + width] = values[:, at : at + width]
            start += width
    for k in range(chips):
        outgoing[k][...] = sorted_cols[meta[CHIP] ^ k]
    for copy in loads[1:]:
        copy.wait()


def backward_kernel(
    d_out, w_out, n_gain, conv_w, a_log, d_skip, mix, slope, xa, dt_wide, y, inv, decay_t, scores_t,
    bc, dt, gate_dt, message, g_conv, d_mixed, through,
):
    f32 = jnp.float32
    seq, inner = xa.shape
    heads = dt.shape[1]
    state = bc.shape[1] // 2
    head_size = inner // heads
    taps = conv_w.shape[0]
    lanes = head_lanes(heads, inner)
    skip = exact_dot(jnp.broadcast_to(d_skip[...], (8, heads)), lanes)[:1]
    scale = inv[:, :1]
    d_norm = lax.dot_general(
        d_out[...], w_out[...], (((1,), (1,)), ((), ())), preferred_element_type=f32
    )
    unit = (y[...] + skip * xa[...]) * scale
    wide = message.shape[1]
    bf16 = jnp.bfloat16
    message[...] = jnp.zeros_like(message)
    g_conv[...] = jnp.zeros_like(g_conv)
    g_conv[taps : taps + 1, :inner] = jnp.sum(d_norm * unit, axis=0, keepdims=True)
    pulled = d_norm * n_gain[...]
    d_mixed[...] = scale * (pulled - unit * jnp.mean(pulled * unit, axis=-1, keepdims=True))

    group = PAIR // head_size
    d_scores_t = jnp.zeros((seq, seq), f32)
    scored = scores_t[...]
    for p in range(inner // PAIR):
        cols = slice(p * PAIR, (p + 1) * PAIR)
        got = d_mixed[:, cols]
        held = dt_wide[:, cols] * xa[:, cols]
        weights = jnp.concatenate(
            [scored * decay_t[h] for h in range(p * group, (p + 1) * group)], axis=1
        )
        through[:, cols] = close_dot(weights, stacked_by_head(got, head_size))
        outer = close_dot(stacked_by_head(held, head_size), got, ((1,), (1,)))
        for i in range(group):
            d_scores_t = d_scores_t + outer[i * seq : (i + 1) * seq] * decay_t[p * group + i]

    d_dt = exact_dot(through[...] * xa[...], lanes, ((1,), (1,)))
    d_running = exact_dot(d_mixed[...] * y[...], lanes, ((1,), (1,))) - dt[...] * d_dt
    row = lax.broadcasted_iota(jnp.int32, (seq, seq), 0)
    col = lax.broadcasted_iota(jnp.int32, (seq, seq), 1)
    later = exact_dot((col >= row).astype(f32), d_running)
    d_step = (d_dt + later * -jnp.exp(a_log[...])) * gate_dt[...]

    for at in range(0, inner, 256):
        cols = slice(at, at + 256)
        d_act = dt_wide[:, cols] * through[:, cols] + skip[:, cols] * d_mixed[:, cols]
        d_conv = d_act * slope[:, cols]
        values = mix[:, cols]
        for k in range(taps):
            g_conv[k : k + 1, cols] = jnp.sum(
                d_conv * delayed(values, taps - 1 - k), axis=0, keepdims=True
            )
    d_b = exact_dot(d_scores_t, bc[:, state:])
    d_c = exact_dot(d_scores_t.T, bc[:, :state])
    for at, d_act in ((0, d_b), (state, d_c)):
        cols = slice(inner + at, inner + at + state)
        d_conv = d_act * slope[:, cols]
        values = mix[:, cols]
        d_mix = d_conv * conv_w[taps - 1 : taps, cols]
        for k in range(taps):
            g_conv[k : k + 1, cols] = jnp.sum(
                d_conv * delayed(values, taps - 1 - k), axis=0, keepdims=True
            )
            if k < taps - 1:
                d_mix = d_mix + advanced(d_conv, taps - 1 - k) * conv_w[k : k + 1, cols]
        message[:seq, at : at + state] = d_mix.astype(bf16)
    message[:seq, 2 * state : 2 * state + heads] = d_step.astype(bf16)
    per_row = (inner + 2 * state) // wide
    packed = [
        g_conv[k : k + 1, i * wide : (i + 1) * wide] for k in range(taps + 1) for i in range(per_row)
    ]
    packed = packed + [jnp.zeros_like(packed[0])] * (TERM_ROWS - len(packed))
    message[seq:, :] = jnp.concatenate(packed).astype(bf16)


def pinned(shape, dtype):
    return pltpu.VMEM(shape, dtype)


def in_vmem(values):
    return [pltpu.with_memory_space_constraint(v, pltpu.VMEM) for v in values]


def student_forward(chips, levels, meta, inputs, loads):
    x, *_, w_x, _, conv_w, dt_bias, _, _, _ = inputs
    seq, width = x.shape
    inner, heads = w_x.shape[1], dt_bias.shape[1]
    both = conv_w.shape[1]
    f32, bf16 = jnp.float32, jnp.bfloat16
    wide = (inner + width) // chips
    shapes = [((seq, wide), bf16)] * chips + [
        ((seq, loads[0].shape[1]), f32),
        ((seq, both), f32), ((seq, both), f32), ((seq, inner), f32), ((seq, inner), f32),
        ((seq, inner), f32), ((seq, 128), f32), ((heads, seq, seq), f32), ((seq, seq), f32),
        ((seq, both - inner), f32), ((seq, heads), f32), ((seq, heads), f32),
    ]
    return pl.pallas_call(
        lambda *refs: forward_kernel(chips, levels, *refs),
        name="student_forward",
        in_specs=[SMEM] + [pl.BlockSpec(memory_space=pltpu.HBM)] * (INPUTS + LOADS),
        out_specs=[VMEM] * (LOADS + len(shapes)),
        out_shape=[pinned(v.shape, v.dtype) for v in loads]
        + [jax.ShapeDtypeStruct(s, t) for s, t in shapes[:chips]]
        + [pinned(s, t) for s, t in shapes[chips:]],
        scratch_shapes=[
            pltpu.VMEM((seq, width), bf16), pltpu.VMEM((seq, inner), bf16),
            pltpu.VMEM((chips, seq, wide), bf16), *[pltpu.VMEM(v.shape, v.dtype) for v in inputs],
            pltpu.SemaphoreType.DMA((INPUTS + LOADS,)),
        ],
        compiler_params=pltpu.CompilerParams(vmem_limit_bytes=15 << 20),
        cost_estimate=NO_COST,
    )(meta, *[pltpu.with_memory_space_constraint(v, pltpu.HBM) for v in (*inputs, *loads)])


def student_backward(d_out, w_out, n_gain, conv_w, a_log, d_skip, saved):
    seq = d_out.shape[0]
    inner, heads = w_out.shape[0], a_log.shape[1]
    both = conv_w.shape[1]
    f32 = jnp.float32
    wide = both // TERM_CHUNKS
    return pl.pallas_call(
        backward_kernel,
        name="student_backward",
        in_specs=[VMEM] * (6 + len(saved)),
        out_specs=VMEM,
        out_shape=jax.ShapeDtypeStruct((seq + TERM_ROWS, wide), jnp.bfloat16),
        scratch_shapes=[
            pltpu.VMEM((8, both), f32), pltpu.VMEM((seq, inner), f32), pltpu.VMEM((seq, inner), f32),
        ],
        compiler_params=pltpu.CompilerParams(vmem_limit_bytes=8 << 20),
        cost_estimate=NO_COST,
    )(d_out, *in_vmem([w_out]), n_gain, conv_w, a_log, d_skip, *in_vmem(saved))


def contract_kernel(count, lanes, extra, meta, *refs):
    cols, blocks = refs[:count], refs[count : 2 * count]
    mine, theirs, part = refs[2 * count :]
    f32 = jnp.float32
    seq = cols[0].shape[0]
    part[...] = lax.dot_general(
        jnp.concatenate([c[:, lanes] for c in cols]),
        jnp.concatenate([b[:seq, :] for b in blocks]),
        (((0,), (0,)), ((), ())),
        preferred_element_type=f32,
    ).reshape(part.shape)
    rows = part.shape[0] * part.shape[2]
    width = part.shape[3]
    mine[:rows, :] = part[:, pl.ds(meta[CORE], 1), :, :].reshape(rows, width)
    theirs[:rows, :] = part[:, pl.ds(1 - meta[CORE], 1), :, :].reshape(rows, width).astype(theirs.dtype)
    if extra:
        total = blocks[0][seq:, :].astype(f32)
        for block in blocks[1:]:
            total = total + block[seq:, :].astype(f32)
        mine[rows:, :] = total
        theirs[rows:, :] = total.astype(theirs.dtype)


def contract(meta, cols, lanes, blocks, levels):
    count = len(cols)
    width = blocks[0].shape[1]
    extra = blocks[0].shape[0] - cols[0].shape[0]
    own = (lanes.stop - lanes.start) // (2 * levels)
    rows = levels * own + extra
    return pl.pallas_call(
        lambda *refs: contract_kernel(count, lanes, extra, *refs),
        name="contract",
        in_specs=[SMEM] + [VMEM] * (2 * count),
        out_specs=[VMEM, VMEM],
        out_shape=[
            jax.ShapeDtypeStruct((rows, width), jnp.float32),
            jax.ShapeDtypeStruct((rows, width), jnp.bfloat16),
        ],
        scratch_shapes=[pltpu.VMEM((levels, 2, own, width), jnp.float32)],
        compiler_params=pltpu.CompilerParams(vmem_limit_bytes=6 << 20),
        cost_estimate=NO_COST,
    )(meta, *cols, *blocks)


def share_kernel(levels, extra, meta, mine_a, got_a, mine_b, got_b, own_a, own_b, *sent):
    f32 = jnp.float32

    def chip_sum(mine, got, at, rows):
        return mine[pl.ds(at, rows), :] + got[pl.ds(at, rows), :].astype(f32)

    rows_a = mine_a.shape[0] // levels
    rows_b = (mine_b.shape[0] - extra) // levels
    width = mine_a.shape[1]
    tail = chip_sum(mine_b, got_b, levels * rows_b, extra)
    for k in range(levels):
        level_at = meta[LEVEL] ^ k
        part_a = chip_sum(mine_a, got_a, pl.multiple_of(level_at * rows_a, rows_a), rows_a)
        part_b = chip_sum(mine_b, got_b, pl.multiple_of(level_at * rows_b, rows_b), rows_b)
        if k == 0:
            own_a[...] = part_a
            own_b[:rows_b, :] = part_b
            own_b[rows_b:, :] = tail
        else:
            to = sent[k - 1]
            if rows_a != rows_b + extra:
                to[...] = jnp.zeros_like(to)
            to[:rows_a, :width] = part_a.astype(to.dtype)
            to[:rows_b, width:] = part_b.astype(to.dtype)
            to[rows_b : rows_b + extra, width:] = tail.astype(to.dtype)


def share(meta, a, b, levels, extra):
    rows_a = a[0].shape[0] // levels
    rows_b = (b[0].shape[0] - extra) // levels + extra
    width_a, width_b = a[0].shape[1], b[0].shape[1]
    f32 = jnp.float32
    return pl.pallas_call(
        lambda *refs: share_kernel(levels, extra, *refs),
        name="share",
        in_specs=[SMEM] + [VMEM] * 4,
        out_specs=[VMEM] * (levels + 1),
        out_shape=[
            jax.ShapeDtypeStruct((rows_a, width_a), f32), jax.ShapeDtypeStruct((rows_b, width_b), f32),
        ]
        + [jax.ShapeDtypeStruct((max(rows_a, rows_b), width_a + width_b), jnp.bfloat16)] * (levels - 1),
        compiler_params=pltpu.CompilerParams(vmem_limit_bytes=4 << 20),
        cost_estimate=NO_COST,
    )(meta, *a, *b)


def finish_kernel(count, taps, meta, own_a, own_b, *refs):
    got = refs[:count]
    g_bcdt, g_conv, g_gain, g_out, terms = refs[count:]
    f32 = jnp.float32
    total = own_a[...]
    rows, width = own_a.shape
    for part in got:
        total = total + part[:rows, :width].astype(f32)
    g_out[...] = total
    total = own_b[...]
    for part in got:
        total = total + part[: own_b.shape[0], width:].astype(f32)
    rows, wide = g_bcdt.shape[0], total.shape[1]
    g_bcdt[...] = total[:rows, : g_bcdt.shape[1]]
    terms[...] = total[rows:, :]
    lane = lax.broadcasted_iota(jnp.int32, (1, wide), 1)

    def window(first, width):
        start = meta[DEVICE] * width
        chunk = start // wide
        offset = start - chunk * wide
        left = pltpu.roll(terms[pl.ds(first + chunk, 1), :], wide - offset, 1)
        right = pltpu.roll(terms[pl.ds(first + chunk + 1, 1), :], wide - offset, 1)
        return jnp.where(lane < wide - offset, left, right)[:, :width]

    g_conv[...] = jnp.concatenate(
        [window(k * TERM_CHUNKS, g_conv.shape[1]) for k in range(taps)]
    )
    g_gain[...] = window(taps * TERM_CHUNKS, g_gain.shape[1])


def finish(meta, own_a, own_b, got, shapes):
    f32 = jnp.float32
    return pl.pallas_call(
        lambda *refs: finish_kernel(len(got), shapes[1][0], *refs),
        name="finish",
        in_specs=[SMEM] + [VMEM] * (2 + len(got)),
        out_specs=[VMEM] * 4,
        out_shape=[jax.ShapeDtypeStruct(s, f32) for s in shapes],
        scratch_shapes=[pltpu.VMEM((TERM_ROWS, own_b.shape[1]), f32)],
        compiler_params=pltpu.CompilerParams(vmem_limit_bytes=3 << 20),
        cost_estimate=NO_COST,
    )(meta, own_a, own_b, *got)


def swap(values):
    size = lax.axis_size("head")
    return lax.ppermute(values, "head", [(i, i ^ 1) for i in range(size)])


def hop(values, step):
    size = lax.axis_size("head")
    return lax.ppermute(values, "head", [(i, i ^ (2 * step)) for i in range(size)])


def level(values, step):
    size = lax.axis_size("series")
    return lax.ppermute(values, "series", [(i, i ^ step) for i in range(size)])


def teacher_kernel(count, meta, *refs):
    pieces = refs[:count]
    gain, w_gate, w_up, readout, proj, mine, theirs, normed, acc = refs[count:]
    f32 = jnp.float32
    feat = proj.shape[0]
    feat_at = pl.multiple_of(meta[HEAD] * feat, feat)
    strip = 16
    start = 0
    for piece in pieces:
        for at in range(0, piece.shape[0], strip):
            values = piece[at : at + strip, :].astype(f32)
            mean_sq = jnp.mean(values * values, axis=-1, keepdims=True)
            scaled = values * lax.rsqrt(mean_sq + EPS) * gain[...]
            normed[start + at : start + at + strip, :] = scaled.astype(jnp.bfloat16)
        acc[start : start + piece.shape[0], :] = jnp.dot(
            piece[:, pl.ds(feat_at, feat)], proj[...], preferred_element_type=f32
        )
        start += piece.shape[0]
    tile = min(256, w_gate.shape[1])
    for at in range(0, w_gate.shape[1], tile):
        cols = slice(at, at + tile)
        gate = jnp.dot(normed[...], w_gate[:, cols], preferred_element_type=f32)
        upward = jnp.dot(normed[...], w_up[:, cols], preferred_element_type=f32)
        hidden = (gate / (1.0 + jnp.exp(-gate)) * upward).astype(jnp.bfloat16)
        acc[...] += jnp.dot(hidden, readout[cols, :], preferred_element_type=f32)
    rows = mine.shape[0]
    mine[...] = acc[:rows, :]
    theirs[...] = acc[rows:, :].astype(jnp.bfloat16)


def teacher_terms(meta, own, other, teacher_gain, w_gate, w_up, readout, proj):
    pieces = own + other
    rows = sum(p.shape[0] for p in own)
    width, out = w_gate.shape[0], readout.shape[1]
    return pl.pallas_call(
        lambda *refs: teacher_kernel(len(pieces), *refs),
        name="teacher",
        in_specs=[SMEM] + [VMEM] * (len(pieces) + 5),
        out_specs=[VMEM, VMEM],
        out_shape=[
            jax.ShapeDtypeStruct((rows, out), jnp.float32),
            jax.ShapeDtypeStruct((rows, out), jnp.bfloat16),
        ],
        scratch_shapes=[
            pltpu.VMEM((2 * rows, width), jnp.bfloat16),
            pltpu.VMEM((2 * rows, out), jnp.float32),
        ],
        compiler_params=pltpu.CompilerParams(vmem_limit_bytes=(5 << 20) + 2 * rows * (2 * width + 6 * out)),
        cost_estimate=NO_COST,
    )(meta, *pieces, teacher_gain.reshape(1, width), *in_vmem([w_gate, w_up, readout, proj]))


def cut_kernel(half, first, second, top, bottom, sems):
    copies = [
        pltpu.make_async_copy(first.at[pl.ds(0, half), :], top, sems.at[0]),
        pltpu.make_async_copy(second.at[pl.ds(half, half), :], bottom, sems.at[1]),
    ]
    for copy in copies:
        copy.start()
    for copy in copies:
        copy.wait()


def halves_to_forward(first, second, half):
    kind = jax.ShapeDtypeStruct((half, first.shape[1]), first.dtype)
    anywhere = pl.BlockSpec(memory_space=pl.ANY)
    return pl.pallas_call(
        lambda *refs: cut_kernel(half, *refs),
        name="cut",
        in_specs=[anywhere, anywhere],
        out_specs=[anywhere, anywhere],
        out_shape=[kind, kind],
        scratch_shapes=[pltpu.SemaphoreType.DMA((2,))],
        compiler_params=pltpu.CompilerParams(vmem_limit_bytes=1 << 20),
        cost_estimate=NO_COST,
    )(first, second)


def per_device(
    teacher_in, teacher_gain, w_gate, w_up, readout, distill_proj, building_ids, student_in,
    embed_rows, covariates, cov_proj, student_gain, w_x, w_bcdt, conv_w, dt_bias, a_log, d_skip,
    norm_gain, w_out,
):
    heads, levels = lax.axis_size("head"), lax.axis_size("series")
    chips = heads // 2
    head, z = lax.axis_index("head"), lax.axis_index("series")
    chip, core = head // 2, head % 2
    seq_len = teacher_in.shape[1]
    series_total = teacher_in.shape[0] * heads * levels
    bf16, f32 = jnp.bfloat16, jnp.float32

    own_rows = teacher_in[0]
    across = [hop(own_rows, k) for k in ((1, 2) if chips == 4 else range(1, chips))]
    meta = jnp.stack([head, core, z, chip, z * heads + head]).astype(jnp.int32)
    emb = lax.dynamic_slice_in_dim(embed_rows, building_ids[0], 1, 0)
    cov = lax.dynamic_slice_in_dim(covariates, building_ids[0], 1, 0)
    meta, emb, cov, w_gate = lax.optimization_barrier((meta, emb, cov, w_gate))
    row = [v.reshape(1, -1) for v in (student_gain, dt_bias, a_log, d_skip, norm_gain)]
    fwd = student_forward(
        chips, levels, meta,
        [
            student_in[0], emb, cov, cov_proj, row[0], w_x, w_bcdt.T, conv_w, row[1], row[2], row[3], row[4],
        ],
        [w_out, w_gate, w_up, readout, distill_proj],
    )
    w_out, w_gate, w_up, readout, distill_proj = fwd[:LOADS]
    fwd = fwd[LOADS:]
    cols, output, saved = list(fwd[:chips]), fwd[chips], fwd[chips + 1 :]
    def teach(own):
        return teacher_terms(
            meta, own, [swap(p) for p in own], teacher_gain, w_gate, w_up, readout, distill_proj
        )

    first = teach([own_rows])
    across, first, cols = lax.optimization_barrier((across, first, cols))

    def settle(terms, steps):
        mine, theirs = terms
        both = mine + swap(theirs).astype(f32)
        blocks = [both[i * seq_len : (i + 1) * seq_len] for i in range(len(steps))]
        return [hop(v.astype(bf16), k) if k else v for v, k in zip(blocks, steps)]

    def exchanged():
        return [cols[0]] + [hop(cols[k], k) for k in range(1, chips)]

    if chips == 4:
        half = seq_len // 2
        top, bottom = halves_to_forward(across[1], across[0], half)
        corner = [hop(top, 1), hop(bottom, 2)]
        second = teach(across)
        corner, second, cols = lax.optimization_barrier((corner, second, cols))
        parts = settle(first, (0,)) + settle(second, (1, 2))
        third = teach(corner)
        cols = exchanged()
        third, cols = lax.optimization_barrier((third, cols))
        parts = parts + settle(third, (3,))
    else:
        cols = exchanged()
        parts = settle(first, (0,))
        for k, v in enumerate(across):
            parts = parts + settle(teach([v]), (k + 1,))
    target = parts[0]
    for part in parts[1:]:
        target = target + part.astype(f32)
    split = w_x.shape[1] // chips

    d_output = ((output - target) / series_total).astype(bf16)
    d_blocks = [d_output] + [hop(d_output, k) for k in range(1, chips)]
    message = student_backward(d_output, w_out, row[4], conv_w, row[2], row[3], saved)
    message, d_blocks[1], cols = lax.optimization_barrier((message, d_blocks[1], cols))
    messages = [message] + [hop(message, k) for k in range(1, chips)]
    first_a, other_a = contract(meta, cols, slice(0, split), d_blocks, levels)
    messages, first_a, other_a = lax.optimization_barrier((messages, first_a, other_a))
    first_b, other_b = contract(meta, cols, slice(split, cols[0].shape[1]), messages, levels)
    own_a, own_b, *sent = share(
        meta, (first_a, swap(other_a)), (first_b, swap(other_b)), levels, TERM_ROWS
    )
    got = [level(v, k + 1) for k, v in enumerate(sent)]

    devices = heads * levels
    g_bcdt, g_conv, g_gain, g_out = finish(
        meta, own_a, own_b, got,
        [
            (w_bcdt.shape[0] // devices, w_bcdt.shape[1]), (conv_w.shape[0], conv_w.shape[1] // devices),
            (1, norm_gain.shape[0] // devices), (w_out.shape[0] // devices, w_out.shape[1]),
        ],
    )
    return (g_bcdt, g_conv, g_gain.reshape(-1), g_out)


def solution(mesh):
    return jax.shard_map(
        per_device,
        mesh=mesh,
        in_specs=(
            P(("series", "head"), None, None),
            P(),
            P(None, "head"),
            P(None, "head"),
            P("head", None),
            P("head", None),
            P(("series", "head")),
            P(("series", "head"), None, None),
            P(),
            P(),
            P(),
            P(),
            P(),
            P(),
            P(),
            P(),
            P(),
            P(),
            P(),
            P(),
        ),
        out_specs=(
            P(("series", "head"), None),
            P(None, ("series", "head")),
            P(("series", "head")),
            P(("series", "head"), None),
        ),
        check_vma=False,
    )
```
